32 devices in a mesh: tm: 8 (over y, x, core), space: 4 (over z).
Axes of the slice: x: 2, y: 2, z: 4, core: 2. Of those that a mesh axis runs over, the one named last changes fastest.
Arguments:
- forcing: float32 [128, 64, 512], P('tm', None, 'space'), may hold values from -1.5 to 1.5
- initial: float32 [64, 512], P(None, 'space'), may hold values from -6 to 6
- blocks: float32 [5, 64, 64], replicated, may hold values from -0.3125 to 0.3125
- coeffs: float32 [5, 512], P(None, 'space'), may hold values from -3 to 3
- damping: float32 [64, 512], P(None, 'space'), may hold values from 1.25 to 2.5
- neighbors: int32 [4, 512], P(None, 'space'), may hold values from 0 to 511, as said below
Outputs:
- solution: float32 [128, 64, 512], P('tm', None, 'space')
The draws below stay inside these ranges and needn't reach their ends.
Inputs may be any that keep to these rules, and one draw needn't show every extreme that they name: neighbors[k, e] = (e + o) mod 512 with 1 <= |o| <= 32; o = 32 and o = -32 both occur; an element may name one neighbour twice.
All inputs are finite; a program needn't handle non-finite values.
Results may differ from the reference program's by a relative error of at most 0.00029.
Values sent between devices are 32-bit elements; how exact they have to be, the bound alone decides.
No kernel may reach another device: no remote copies, remote signals or barrier semaphores. Data moves between devices by JAX's collectives and lax.ppermute only.
A program may use at most 64 MiB of HBM per device.

```python
import math
import jax
import jax.numpy as jnp
from jax import lax

BV = 64
FACES = 4
KB = 5
REACH = 32
CF = 4
LEVELS = 3
CYCLES = 2
NT = 128
NE = 512


def draw_neighbors(key, part):
    offsets = jax.random.randint(key, (FACES, NE), 0, 2 * REACH)
    offsets = jnp.where(offsets < REACH, offsets - REACH, offsets - REACH + 1)
    offsets = offsets.at[0, 0].set(REACH).at[0, 1].set(-REACH)
    elements = jnp.arange(NE, dtype=jnp.int32)[None, :]
    return ((elements + offsets) % NE).astype(jnp.int32)


def steps_of(stream_key, extent, cuts, low, top_value):
    def one(axis_at, shards_of):
        heights = jax.random.uniform(jax.random.fold_in(jax.random.fold_in(stream_key, 6), axis_at), (shards_of,), jnp.float32, low / len(cuts), top_value / len(cuts))
        return jnp.repeat(jnp.exp(heights), extent[axis_at] // shards_of).reshape((-1,) + (1,) * (len(extent) - axis_at - 1))

    gain = one(*cuts[0])
    for cut in cuts[1:]:
        gain = gain * one(*cut)
    return gain


def gaussian(own_key, extent, spread, most, cuts=(), kind=jnp.bfloat16):
    loudness = steps_of(own_key, extent, cuts, -0.22, 0.18) if cuts else 1.0
    entries = jax.random.normal(own_key, extent, jnp.float32) * spread * loudness
    return jnp.minimum(jnp.maximum(entries, -most), most).astype(kind)


def setup_inputs(seed: int = 0) -> dict:
    seeds = jax.random.split(jax.random.key(seed), 7)
    forcing = gaussian(seeds[0], (NT, BV, NE), 0.25, 1.5, ((0, 8), (2, 4)), jnp.float32)
    initial = gaussian(seeds[1], (BV, NE), 1.0, 6.0, ((1, 4),), jnp.float32)
    blocks = gaussian(seeds[2], (KB, BV, BV), (KB * BV) ** -0.5, 0.3125, (), jnp.float32)
    coeffs = gaussian(seeds[3], (KB, NE), 1.0, 3.0, ((1, 4),), jnp.float32)
    damping = jnp.clip(jnp.exp(math.log(2.5) - 0.6931472 * jax.random.uniform(seeds[4], (BV, NE), jnp.float32) ** steps_of(seeds[4], (BV, NE), ((1, 4),), -0.2, 0.2)), 1.25, 2.5)
    neighbors = draw_neighbors(jax.random.fold_in(seeds[6], 71), 0)
    return dict(forcing=forcing, initial=initial, blocks=blocks, coeffs=coeffs, damping=damping, neighbors=neighbors)


time_step = 0.015625


def advance(fields, stride, operator):
    blocks, coeffs, damping, columns = operator
    picked = jnp.take(fields, columns.reshape(-1), axis=2)
    picked = picked.reshape(fields.shape[0], fields.shape[1], columns.shape[0], columns.shape[1])
    picked = picked * coeffs[None, None, :, :]
    coupled = jnp.einsum("kab,tbke->tae", blocks, picked, precision=lax.Precision.HIGHEST)
    return fields + stride * (coupled - damping[None] * fields)


def relax_f(values, sources, start_state, stride, operator):
    intervals = values.shape[0] // CF
    shaped = values.reshape((intervals, CF) + values.shape[1:])
    shaped_src = sources.reshape((intervals, CF) + sources.shape[1:])
    previous = jnp.concatenate([start_state[None], shaped[:-1, CF - 1]], axis=0)
    pieces = []
    for offset in range(CF - 1):
        previous = advance(previous, stride, operator) + shaped_src[:, offset]
        pieces.append(previous)
    pieces.append(shaped[:, CF - 1])
    return jnp.stack(pieces, axis=1).reshape(values.shape)


def relax_c(values, sources, stride, operator):
    intervals = values.shape[0] // CF
    shaped = values.reshape((intervals, CF) + values.shape[1:])
    shaped_src = sources.reshape((intervals, CF) + sources.shape[1:])
    c_point = advance(shaped[:, CF - 2], stride, operator) + shaped_src[:, CF - 1]
    return jnp.concatenate([shaped[:, :CF - 1], c_point[:, None]], axis=1).reshape(values.shape)


def restrict(values, sources, stride, operator):
    intervals = values.shape[0] // CF
    shaped = values.reshape((intervals, CF) + values.shape[1:])
    shaped_src = sources.reshape((intervals, CF) + sources.shape[1:])
    return shaped_src[:, CF - 1] + advance(shaped[:, CF - 2], stride, operator) - shaped[:, CF - 1]


def correct(values, correction):
    intervals = values.shape[0] // CF
    shaped = values.reshape((intervals, CF) + values.shape[1:])
    updated = shaped[:, CF - 1] + correction
    return jnp.concatenate([shaped[:, :CF - 1], updated[:, None]], axis=1).reshape(values.shape)


def vcycle(values, sources, start_state, level_index, operator):
    stride = time_step * CF ** level_index
    if level_index == LEVELS - 1:
        def march(carried, source):
            carried = advance(carried[None], stride, operator)[0] + source
            return carried, carried

        final_state, solved = lax.scan(march, start_state, sources)
        return solved
    values = relax_f(values, sources, start_state, stride, operator)
    values = relax_c(values, sources, stride, operator)
    values = relax_f(values, sources, start_state, stride, operator)
    residual = restrict(values, sources, stride, operator)
    correction = vcycle(jnp.zeros_like(residual), residual, jnp.zeros_like(start_state), level_index + 1, operator)
    values = correct(values, correction)
    return relax_f(values, sources, start_state, stride, operator)


def reference(forcing, initial, blocks, coeffs, damping, neighbors):
    own_cols = jnp.arange(NE, dtype=jnp.int32)[None, :]
    columns = jnp.concatenate([own_cols, neighbors.astype(jnp.int32)], axis=0)
    operator = (blocks, coeffs, damping, columns)
    values = jnp.zeros(forcing.shape, jnp.float32)
    for cycle_index in range(CYCLES):
        values = vcycle(values, forcing, initial, 0, operator)
    return values
```

```python
import functools

import jax
import jax.numpy as jnp
from jax import lax
from jax.experimental import pallas as pl
from jax.experimental.pallas import tpu as pltpu
from jax.sharding import PartitionSpec

F32 = jnp.float32
BF16 = jnp.bfloat16
BV = 64
LANES = 128
S0 = 0.015625
S1 = S0 * 4
S2 = S0 * 16
PAR = 80
VMEM_LIMIT = 60 * 1024 * 1024


def split(x):
    hi = x.astype(BF16)
    return hi, (x - hi.astype(F32)).astype(BF16)


class Node:
    def __init__(self, plan, terms, s, tiles):
        self.terms, self.s, self.tiles = terms, s, tiles
        self.level = 1 + max([t.level for _, t in terms] + [0])
        plan.nodes.append(self)
        plan.depth = max(plan.depth, self.level)


class Input:
    level = 0

    def __init__(self, get):
        self.get = get


def lin(*terms):
    flat = []
    for c, v in terms:
        if isinstance(v, list):
            flat += [(c * d, n) for d, n in v]
        else:
            flat.append((c, v))
    merged = []
    for c, v in flat:
        for i, (d, n) in enumerate(merged):
            if n is v:
                merged[i] = (c + d, n)
                break
        else:
            merged.append((c, v))
    return [(c, n) for c, n in merged if c != 0]


class Plan:
    def __init__(self, count):
        self.nodes, self.depth, self.count = [], 0, count

    def apply(self, x, s, tiles=None):
        if not isinstance(x, list):
            x = [(1.0, x)]
        return Node(self, x, s, tiles)

    def power(self, x, s, n, tiles=None):
        for _ in range(n):
            x = self.apply(x, s, tiles)
        return x

    def schedule(self, finals):
        used = {}
        for n in reversed(self.nodes):
            latest = self.depth
            for u in used.get(id(n), []):
                latest = min(latest, u.level - 1)
            n.level = latest
            for _, t in n.terms:
                used.setdefault(id(t), []).append(n)
        final_ids = {id(n) for n in finals}
        self.levels = [[n for n in self.nodes if n.level == l] for l in range(1, self.depth + 1)]
        self.levels = [l for l in self.levels if l]
        free, total = [], 0
        for nodes in self.levels:
            for n in self.nodes:
                if hasattr(n, "slot") and not getattr(n, "freed", False) and id(n) not in final_ids:
                    last = max([u.level for u in used.get(id(n), [])] + [n.level])
                    if last <= nodes[0].level:
                        n.freed = True
                        free.append(n.slot)
            for n in nodes:
                if free:
                    n.slot = free.pop()
                else:
                    n.slot = total
                    total += 1
        self.total = total
        self.width = max(len(l) for l in self.levels)


def build_operator(par_get, count, s_ref, cf_ref, d_ref):
    rows = lax.broadcasted_iota(jnp.int32, (256, LANES), 0)
    for t in range(count):
        par = par_get(t)
        d_ref[t] = par[:BV]
        cf_ref[t] = par[BV : BV + 8]
        for k in range(4):
            code = par[BV + 8 + k : BV + 9 + k].astype(jnp.int32)
            s_ref[t, :, LANES * k : LANES * (k + 1)] = jnp.where(rows == code, 1.0, 0.0).astype(BF16)


def value(terms, t, buf):
    total = None
    for c, v in terms:
        x = buf[v.slot, t] if isinstance(v, Node) else v.get(t)
        x = x if c == 1.0 else c * x
        total = x if total is None else total + x
    return total


def run_level(nodes, ring, op, buf, xbuf):
    s_ref, cf_ref, d_ref, w_ref = op
    count = len(ring)
    batch = len(nodes)
    lane = lax.broadcasted_iota(jnp.int32, (BV, LANES), 1)
    looped = count > 4

    def spread(x):
        hi, lo = split(x)
        return jnp.concatenate([hi, lo], axis=0)

    half = lax.broadcasted_iota(jnp.int32, (2 * BV, LANES), 1) < 64

    def couple(xs, near, tiles):
        blocks, out = [], {}
        for i, t in enumerate(tiles):
            stack = []
            for b in range(batch):
                right, left = near(b, t)
                edge = jnp.where(half, right.astype(F32), left.astype(F32)).astype(BF16)
                stack.append(jnp.concatenate([xs(b, t), edge], axis=1))
            got = jnp.dot(jnp.concatenate(stack, axis=0), s_ref[t], preferred_element_type=F32)
            for b in range(batch):
                pick = got[2 * BV * b : 2 * BV * b + BV] + got[2 * BV * b + BV : 2 * BV * (b + 1)]
                own = xs(b, t)
                own = own[:BV].astype(F32) + own[BV:].astype(F32)
                cf = cf_ref[t]
                col = [own * cf[0:1]] + [pick[:, LANES * k : LANES * (k + 1)] * cf[k + 1 : k + 2] for k in range(4)]
                blocks.append(((b, i), col))
        for i in range(0, len(blocks), 2):
            pair = blocks[i : i + 2]
            if len(pair) == 2:
                cols = [jnp.concatenate([u, v], axis=1) for u, v in zip(pair[0][1], pair[1][1])]
            else:
                cols = pair[0][1]
            hi, lo = split(jnp.concatenate(cols, axis=0))
            o = jnp.dot(w_ref[...], jnp.concatenate([hi, lo], axis=0), preferred_element_type=F32)
            o = o[:BV] + o[BV:]
            for q, (key, _) in enumerate(pair):
                out[key] = o[:, LANES * q : LANES * (q + 1)]
        return out

    if not looped:
        x = {(b, t): value(n.terms, t, buf) for b, n in enumerate(nodes) for t in ring}
        sp = {key: spread(v) for key, v in x.items()}
        at = {t: i for i, t in enumerate(ring)}
        wanted = [t for t in ring if any(n.tiles is None or t in n.tiles for n in nodes)]
        out = couple(
            lambda b, t: sp[b, t],
            lambda b, t: (sp[b, ring[(at[t] + 1) % count]], sp[b, ring[(at[t] - 1) % count]]),
            wanted,
        )
        for (b, i), v in out.items():
            t = wanted[i]
            y = x[b, t] + nodes[b].s * (v - d_ref[t] * x[b, t])
            buf[nodes[b].slot, t] = y
        return

    @pl.loop(0, count)
    def _(t):
        for b, n in enumerate(nodes):
            xbuf[b, t] = value(n.terms, t, buf)

    @pl.loop(0, count)
    def _(t):
        right = lax.rem(t + 1, count)
        left = lax.rem(t + count - 1, count)
        out = couple(
            lambda b, u: spread(xbuf[b, u]),
            lambda b, u: (spread(xbuf[b, right]), spread(xbuf[b, left])),
            [t],
        )
        for b, n in enumerate(nodes):
            x = xbuf[b, t]
            buf[n.slot, t] = x + n.s * (out[b, 0] - d_ref[t] * x)


def run(plan, op, buf, xbuf):
    for nodes in plan.levels:
        ring = list(range(plan.count))
        if plan.count <= 4 and all(n.tiles is not None for n in nodes):
            ring = [t for t in ring if t in set().union(*[n.near for n in nodes])]
        run_level(nodes, ring, op, buf, xbuf)


def scratch_for(plan):
    t = plan.count
    return [
        pltpu.VMEM((t, 256, 4 * LANES), BF16),
        pltpu.VMEM((t, 8, LANES), F32),
        pltpu.VMEM((t, BV, LANES), F32),
        pltpu.VMEM((plan.total, t, BV, LANES), F32),
        pltpu.VMEM((plan.width if t > 4 else 1, t if t > 4 else 1, BV, LANES), F32),
    ]


def call(kernel, outs, scratch, smem, args, flops=1):
    specs = [pl.BlockSpec(memory_space=pltpu.SMEM)] * smem
    specs += [pl.BlockSpec(memory_space=pltpu.VMEM)] * (len(args) - smem)
    single = not isinstance(outs, (list, tuple))
    shapes = [outs] if single else list(outs)
    res = pl.pallas_call(
        kernel,
        out_shape=shapes,
        in_specs=specs,
        out_specs=[pl.BlockSpec(memory_space=pltpu.VMEM)] * len(shapes),
        scratch_shapes=scratch,
        compiler_params=pltpu.CompilerParams(vmem_limit_bytes=VMEM_LIMIT),
        cost_estimate=pl.CostEstimate(flops=flops, bytes_accessed=1 << 20, transcendentals=0),
    )(*args)
    return res[0] if single else res


def shape(*dims, dtype=F32):
    return jax.ShapeDtypeStruct(dims, dtype)


def pack_kernel(pos, b, w0, blocks, coeffs, damping, neighbors, up, dn, par, wcat):
    lane = lax.broadcasted_iota(jnp.int32, (BV, LANES), 1)
    nb = neighbors[...]
    low = jnp.bitwise_and(nb, LANES - 1)
    tile = lax.shift_right_logical(nb, 7)
    code = jnp.where(tile == pos[1], low, low + LANES).astype(F32)
    p = jnp.concatenate(
        [damping[...], coeffs[...], jnp.zeros((3, LANES), F32), code, jnp.zeros((4, LANES), F32)], axis=0
    )
    par[...] = p
    for ref in (up, dn):
        ref[0:PAR] = p
        ref[PAR : PAR + BV] = w0[...]
    base = PAR + BV
    for i in range(4):
        r = slice(base + BV * i, base + BV * (i + 1))
        up[r] = jnp.where(lane >= 32, b[4 * i], pltpu.roll(b[4 * i + 2], 32, 1))
        dn[r] = jnp.where(lane < 96, b[4 * i], pltpu.roll(b[4 * i + 2], 96, 1))
    for h in range(2):
        r = slice(base + BV * (4 + h), base + BV * (5 + h))
        other = pltpu.roll(b[8 * h + 5], 64, 1)
        up[r] = jnp.where(lane >= 64, b[8 * h + 1], other)
        dn[r] = jnp.where(lane < 64, b[8 * h + 1], other)
    w = jnp.concatenate([blocks[k] for k in range(5)], axis=1)
    hi, lo = split(w)
    top = jnp.concatenate([hi.astype(F32), hi.astype(F32)], axis=1)
    bot = jnp.concatenate([lo.astype(F32), jnp.zeros_like(w)], axis=1)
    wcat[...] = jnp.concatenate([top, bot], axis=0).astype(BF16)


def fine_plan():
    plan = Plan(3)
    bs = [[Input(None) for _ in range(3)] for _ in range(4)]
    w0 = Input(None)
    first = plan.apply(w0, S0)
    outs = []
    for i in range(4):
        f0 = lin((1.0, bs[i][0]), *([(1.0, first)] if i == 0 else []))
        f1 = lin((1.0, plan.apply(f0, S0)), (1.0, bs[i][1]))
        f2 = lin((1.0, plan.apply(f1, S0)), (1.0, bs[i][2]))
        q3 = plan.apply(f2, S0, {0})
        q3.near = {0, 1, 2}
        outs.append((f0, f1, f2, q3))
    plan.schedule([n for o in outs for f in o for _, n in (f if isinstance(f, list) else [(1, f)]) if isinstance(n, Node)])
    return plan, bs, w0, outs


def fine_kernel(pos, b, w0, par, left, right, wcat, g, f, s_ref, cf_ref, d_ref, buf, xbuf):
    plan, bs, w_in, outs = fine_plan()
    src = [par, right, left]
    build_operator(lambda t: src[t][0:PAR], 3, s_ref, cf_ref, d_ref)
    base = PAR + BV

    def get(i, m, t):
        if t == 0:
            return b[4 * i + m]
        ref = (None, right, left)[t]
        if m == 1:
            x = ref[base + BV * (4 + i // 2) : base + BV * (5 + i // 2)]
            return pltpu.roll(x, 64, 1) if i % 2 else x
        x = ref[base + BV * i : base + BV * (i + 1)]
        if m == 0:
            return x
        return pltpu.roll(x, 32 if t == 1 else 96, 1)

    for i in range(4):
        for m in range(3):
            bs[i][m].get = functools.partial(get, i, m)
    on = jnp.where(pos[0] == 0, 1.0, 0.0).astype(F32)
    w_in.get = lambda t: on * (w0[...] if t == 0 else src[t][PAR : PAR + BV])
    run(plan, (s_ref, cf_ref, d_ref, wcat), buf, xbuf)
    for i in range(4):
        f0, f1, f2, q3 = outs[i]
        f[i] = value(f0, 0, buf)
        f[4 + i] = value(f1, 0, buf)
        f[8 + i] = value(f2, 0, buf)
        g[i] = buf[q3.slot, 0] + b[4 * i + 3]


def tiles_of(refs, stacked):
    if stacked:
        return lambda t, *ix: refs[0][(t, *ix)]
    return lambda t, *ix: refs[t][ix]


def middle_plan(count):
    plan = Plan(count)
    g = [Input(None) for _ in range(5)]
    gm2, gm1, g0, g1, g2 = g
    t = lin((1.0, plan.apply(gm1, S1)), (1.0, g0))
    a = lin((1.0, plan.apply(t, S1)), (1.0, g1))
    k = lin((1.0, plan.apply(a, S1)), (1.0, g2))
    r = lin((2.0, gm1), (-1.0, plan.apply(gm2, S1)))
    p = lin((1.0, plan.apply(r, S1)), (1.0, g0))
    plan.schedule([n for f in (a, k, p) for _, n in f if isinstance(n, Node)])
    return plan, g, (k, p, a)


def each_tile(count, body):
    if count <= 4:
        for t in range(count):
            body(t)
    else:
        pl.loop(0, count)(body)


def middle_kernel(count, n_src, prev, wcat, *refs):
    par_refs, g_refs = refs[:n_src], refs[n_src : 2 * n_src]
    kp, a_out, s_ref, cf_ref, d_ref, buf, xbuf = refs[2 * n_src :]
    stacked = n_src == 1 and count > 1
    plan, g, (k, p, a) = middle_plan(count)
    par_at = tiles_of(par_refs, stacked)
    g_at = tiles_of(g_refs, stacked)
    build_operator(lambda t: par_at(t, slice(0, PAR)), count, s_ref, cf_ref, d_ref)
    g[0].get = lambda t: prev[t, 0]
    g[1].get = lambda t: prev[t, 1]
    for i in range(3):
        g[2 + i].get = functools.partial(lambda i, t: g_at(t, i), i)
    run(plan, (s_ref, cf_ref, d_ref, wcat), buf, xbuf)

    def store(t):
        kp[0, 0, t] = value(k, t, buf)
        kp[0, 1, t] = value(p, t, buf)
        a_out[t] = value(a, t, buf)

    each_tile(count, store)


def final_plan(count, n_tm):
    plan = Plan(count)
    ks = {n: Input(None) for n in range(1, n_tm)}
    ps = {n: Input(None) for n in range(1, n_tm)}
    gm2, gm1, g0, g1, g2, g3 = gs = [Input(None) for _ in range(6)]
    a = Input(None)
    P = lambda x, n=1, tiles=None: plan.power(x, S0, n, tiles)
    Q = lambda x, n=1: plan.power(x, S1, n)
    R = lambda x: plan.apply(x, S2)
    top = n_tm - 1
    delta = {top - 1: lin((1.0, ks[top]))}
    deltap = {}
    pi = lin((1.0, ps[top]))
    for n in range(top - 1, 1, -1):
        if n - 1 > 1:
            if n in deltap:
                deltap[n - 1] = lin((1.0, R(deltap[n])), (1.0, delta[n]))
            else:
                deltap[n - 1] = delta[n]
        delta[n - 1] = lin((1.0, R(delta[n])), (1.0, ks[n]))
        pi = lin((1.0, R(pi)), (1.0, ps[n]))
    theta = {n: lin((1.0, ks[n]), (1.0, Q(delta[n], 4))) for n in (1, 2, 3)}
    thetap = {n: lin((1.0, delta[n]), (1.0, Q(deltap[n], 4))) for n in (2, 3)}
    q1 = Q(thetap[2])
    q3t = Q(q1, 2)
    mid = Q(lin((1.0, Q(thetap[3], 4)), (3.0, thetap[2]), (1.0, delta[2])), 2)
    d2 = lin((1.0, P(lin((1.0, mid), (1.0, pi)), 4)), (-1.0, Q(pi)), (-4.0, q3t))
    q3 = Q(theta[2], 3)
    mid = Q(lin((1.0, Q(theta[3], 4)), (3.0, theta[2]), (1.0, ks[2])), 2)
    m = lin((1.0, P(lin((1.0, mid), (1.0, ps[1])), 4)), (-1.0, Q(ps[1])), (-4.0, q3))
    q4d2 = Q(d2, 4)
    v = lin((1.0, m), (1.0, q4d2))
    v0 = lin((1.0, a), (1.0, q3), (1.0, v))
    psi_a = lin((1.0, P(a, 4)), (-1.0, Q(a)))
    v1 = lin((1.0, P(q3, 4)), (1.0, ks[1]), (1.0, Q(v)), (1.0, psi_a))
    h = lin((1.0, v1), (-1.0, theta[1]))
    qh = Q(h)
    pt, qt = P(theta[1], 4), Q(theta[1])
    pg0, qg0, pg1 = P(gm1, 4), Q(gm1), P(g0, 4)
    v2 = lin((1.0, gm1), (1.0, pt), (1.0, qh))
    v3 = lin((1.0, g0), (1.0, pg0), (1.0, Q(lin((2.0, pt), (-1.0, qt), (1.0, qh)))))
    inner = Q(lin((3.0, pt), (-2.0, qt), (1.0, qh)))
    v4 = lin(
        (1.0, g1),
        (1.0, pg1),
        (1.0, Q(lin((2.0, pg0), (-1.0, qg0), (1.0, inner)))),
        (1.0, R(q4d2)),
        (-1.0, Q(q4d2, 4)),
    )
    near = {0, 1, count - 1} if count == 4 else None

    def P_near(x, tiles):
        y = plan.apply(x, S0, tiles)
        if tiles is not None:
            y.near = near
        return y

    own = {0} if near else None
    c2 = []
    for n, x in enumerate((v0, v1, v2, v3, v4)):
        y = lin((1.0, P(x, 4)), (1.0, gs[n]))
        y = P(y, 2)
        y = P_near(P_near(y, near), near)
        c2.append(lin((1.0, y), (1.0, gs[n + 1])))
    hom = []
    for n in range(4):
        y1 = P_near(c2[n], near)
        y2 = P_near(y1, near)
        y3 = P_near(y2, own)
        hom.append((y1, y2, y3))
    finals = [n for y in hom for n in y] + [n for c in c2 for _, n in c if isinstance(n, Node)]
    plan.schedule(finals)
    return plan, ks, ps, gs, a, c2, hom


def final_kernel(count, n_tm, n_src, pos, held, got, prev, aprev, f, wcat, *refs):
    par_refs, g_refs = refs[:n_src], refs[n_src : 2 * n_src]
    out, kbuf, s_ref, cf_ref, d_ref, buf, xbuf = refs[2 * n_src :]
    stacked = n_src == 1 and count > 1
    plan, ks, ps, gs, a, c2, hom = final_plan(count, n_tm)
    par_at = tiles_of(par_refs, stacked)
    g_at = tiles_of(g_refs, stacked)
    build_operator(lambda t: par_at(t, slice(0, PAR)), count, s_ref, cf_ref, d_ref)
    j = pos[0]
    for n in range(1, n_tm):
        owner = j - n
        on = jnp.where(owner >= 0, 1.0, 0.0).astype(F32)
        slot, far = slot_of(j, jnp.maximum(owner, 0))

        def load(t, n=n, on=on, slot=slot, far=far):
            for i in range(2):
                x = jnp.where(far == 1, got[slot, i, t], held[slot, i, t])
                kbuf[n - 1, i, t] = on * x

        each_tile(count, load)
        ks[n].get = functools.partial(lambda n, t: kbuf[n - 1, 0, t], n)
        ps[n].get = functools.partial(lambda n, t: kbuf[n - 1, 1, t], n)
    gs[0].get = lambda t: prev[t, 0]
    gs[1].get = lambda t: prev[t, 1]
    for i in range(4):
        gs[2 + i].get = functools.partial(lambda i, t: g_at(t, i), i)
    a.get = lambda t: aprev[t]
    run(plan, (s_ref, cf_ref, d_ref, wcat), buf, xbuf)
    for n in range(4):
        for m in range(3):
            out[4 * n + m] = f[4 * m + n] + buf[hom[n][m].slot, 0]
        out[4 * n + 3] = value(c2[n + 1], 0, buf)


MASKS = ((2, 4), (4, 2), (1, 1))


def slot_of(j, owner):
    r = jnp.bitwise_xor(j, owner)
    far = jnp.bitwise_and(r, 1)
    odd = jnp.bitwise_and(owner, 1)
    b1 = jnp.bitwise_and(lax.shift_right_logical(r, 1), 1)
    b2 = jnp.bitwise_and(lax.shift_right_logical(r, 2), 1)
    return jnp.where(odd == 1, b2 + 2 * b1, b1 + 2 * b2), far


def shards(forcing, initial, blocks, coeffs, damping, neighbors):
    n_tm, n_sp = lax.axis_size("tm"), lax.axis_size("space")
    count = n_sp
    tm, sp = lax.axis_index("tm"), lax.axis_index("space")
    pos = jnp.stack([tm, sp]).astype(jnp.int32)

    def around(x, r):
        return lax.ppermute(x, "space", [((i + r) % n_sp, i) for i in range(n_sp)])

    def relative(x):
        if n_sp <= 4:
            return [x] + [around(x, r) for r in range(1, n_sp)]
        every = lax.all_gather(x, "space", axis=0)
        return [jnp.roll(every, -sp, axis=0)]

    halo = PAR + BV + 6 * BV
    up, dn, par, wcat = call(
        pack_kernel,
        [shape(halo, LANES), shape(halo, LANES), shape(PAR, LANES), shape(2 * BV, 640, dtype=BF16)],
        [],
        1,
        (pos, forcing, initial, blocks, coeffs, damping, neighbors),
    )
    left, right = around(up, -1), around(dn, 1)
    plan = fine_plan()[0]
    g, f = call(
        fine_kernel,
        [shape(4, BV, LANES), shape(12, BV, LANES)],
        scratch_for(plan),
        1,
        (pos, forcing, initial, par, left, right, wcat),
    )
    if n_sp == 4:
        pars = [par, right, around(par, 2), left]
    else:
        pars = relative(par)
    gs = relative(g)
    n_src = len(gs)
    late = jnp.stack([x[2:4] for x in gs]) if n_src > 1 else gs[0][:, 2:4]
    chain = [(i, i + 1) for i in range(n_tm - 1)]
    prev = lax.ppermute(late, "tm", chain)
    plan = middle_plan(count)[0]
    kp, a = call(
        functools.partial(middle_kernel, count, n_src),
        [shape(1, 2, count, BV, LANES), shape(count, BV, LANES)],
        scratch_for(plan),
        0,
        (prev, wcat, *pars, *gs),
    )
    held = kp
    for even, odd in MASKS[:2]:
        perm = [(i, i ^ (odd if i % 2 else even)) for i in range(n_tm)]
        held = jnp.concatenate([held, lax.ppermute(held, "tm", perm)], axis=0)
    got = lax.ppermute(held, "tm", [(i, i ^ 1) for i in range(n_tm)])
    aprev = lax.ppermute(a, "tm", chain)
    plan = final_plan(count, n_tm)[0]
    return call(
        functools.partial(final_kernel, count, n_tm, n_src),
        shape(16, BV, LANES),
        [pltpu.VMEM((n_tm - 1, 2, count, BV, LANES), F32)] + scratch_for(plan),
        1,
        (pos, held, got, prev, aprev, f, wcat, *pars, *gs),
    )


def solution(mesh):
    spec = PartitionSpec
    in_specs = (
        spec("tm", None, "space"),
        spec(None, "space"),
        spec(),
        spec(None, "space"),
        spec(None, "space"),
        spec(None, "space"),
    )
    return jax.shard_map(
        shards, mesh=mesh, in_specs=in_specs, out_specs=spec("tm", None, "space"), check_vma=False
    )
```

```python
import functools

import jax
import jax.numpy as jnp
from jax import lax
from jax.experimental import pallas as pl
from jax.experimental.pallas import tpu as pltpu
from jax.sharding import PartitionSpec

F32 = jnp.float32
BF16 = jnp.bfloat16
BV = 64
LANES = 128
S0 = 0.015625
S1 = S0 * 4
S2 = S0 * 16
PAR = 80
FILL = 4
VMEM_LIMIT = 60 * 1024 * 1024


def split(x):
    hi = x.astype(BF16)
    return hi, (x - hi.astype(F32)).astype(BF16)


class Node:
    def __init__(self, plan, terms, s, tiles, parts, keep):
        self.terms, self.s, self.tiles, self.parts, self.keep = terms, s, tiles, parts, keep
        self.level = 1 + max([t.level for _, t in terms] + [0])
        self.done = False
        plan.nodes.append(self)
        plan.depth = max(plan.depth, self.level)


class Input:
    level = 0

    def __init__(self, get):
        self.get = get


def lin(*terms):
    flat = []
    for c, v in terms:
        if isinstance(v, list):
            flat += [(c * d, n) for d, n in v]
        else:
            flat.append((c, v))
    merged = []
    for c, v in flat:
        for i, (d, n) in enumerate(merged):
            if n is v:
                merged[i] = (c + d, n)
                break
        else:
            merged.append((c, v))
    return [(c, n) for c, n in merged if c != 0]


class Plan:
    def __init__(self, count):
        self.nodes, self.depth, self.count = [], 0, count

    def apply(self, x, s, parts=1, tiles=None, keep=True):
        if not isinstance(x, list):
            x = [(1.0, x)]
        return Node(self, x, s, tiles, parts, keep)

    def power(self, x, s, n, parts=1):
        for _ in range(n):
            x = self.apply(x, s, parts)
        return x

    def excess(self, x, s):
        part = lambda y: self.apply(y, s, keep=False)
        y = part(lin((4.0, x), (1.0, part(x))))
        return part(part(lin((6.0, x), (1.0, y))))

    def schedule(self, finals):
        used = {}
        for n in reversed(self.nodes):
            n.latest = self.depth
            for u in used.get(id(n), []):
                n.latest = min(n.latest, u.latest - 1)
            for _, t in n.terms:
                used.setdefault(id(t), []).append(n)
        final_ids = {id(n) for n in finals}
        todo, self.levels = list(self.nodes), []
        for level in range(1, self.depth + 1):
            ready = [n for n in todo if all(isinstance(t, Input) or t.done for _, t in n.terms)]
            ready.sort(key=lambda n: n.latest)
            now = [n for i, n in enumerate(ready) if n.latest == level or i < FILL]
            for n in now:
                n.level = level
            todo = [n for n in todo if n not in now]
            self.levels.append(now)
            for n in now:
                n.done = True
        free, total = [], 0
        for nodes in self.levels:
            for n in self.nodes:
                if hasattr(n, "slot") and not getattr(n, "freed", False) and id(n) not in final_ids:
                    last = max([u.level for u in used.get(id(n), [])] + [n.level])
                    if last <= nodes[0].level:
                        n.freed = True
                        free.append(n.slot)
            for n in nodes:
                if free:
                    n.slot = free.pop()
                else:
                    n.slot = total
                    total += 1
        self.total = total
        self.width = max(len(l) for l in self.levels)


def build_operator(par_get, count, s_ref, cf_ref, d_ref):
    rows = lax.broadcasted_iota(jnp.int32, (256, LANES), 0)
    for t in range(count):
        par = par_get(t)
        d_ref[t] = par[:BV]
        cf_ref[t] = par[BV : BV + 8]
        for k in range(4):
            code = par[BV + 8 + k : BV + 9 + k].astype(jnp.int32)
            s_ref[t, :, LANES * k : LANES * (k + 1)] = jnp.where(rows == code, 1.0, 0.0).astype(BF16)


def value(terms, t, buf):
    total = None
    for c, v in terms:
        x = buf[v.slot, t] if isinstance(v, Node) else v.get(t)
        x = x if c == 1.0 else c * x
        total = x if total is None else total + x
    return total


def unique(items):
    seen = []
    for t in items:
        if not any(t is u for u in seen):
            seen.append(t)
    return seen


def run_level(nodes, ring, op, buf, xbuf):
    s_ref, cf_ref, d_ref, w_ref = op
    count = len(ring)
    lane = lax.broadcasted_iota(jnp.int32, (BV, LANES), 1)
    parts = [n.parts for n in nodes]

    def couple(at, near, blocks):
        columns = {1: [], 2: []}
        for t in unique(t for _, t in blocks):
            here = [b for b, u in blocks if u is t]
            stack = []
            for b in here:
                right, left = near(b, t)
                x = jnp.concatenate([at(b, t), jnp.where(lane < 64, right, left)], axis=1)
                stack += list(split(x)) if parts[b] == 2 else [x.astype(BF16)]
            got = jnp.dot(jnp.concatenate(stack, axis=0), s_ref[t], preferred_element_type=F32)
            cf, row = cf_ref[t], 0
            for b in here:
                pick = got[row : row + BV]
                if parts[b] == 2:
                    pick = pick + got[row + BV : row + 2 * BV]
                row += BV * parts[b]
                col = [at(b, t) * cf[0:1]]
                col += [pick[:, LANES * k : LANES * (k + 1)] * cf[k + 1 : k + 2] for k in range(4)]
                columns[parts[b]].append(((b, t), col))
        out = []
        for part, cols in columns.items():
            for i in range(0, len(cols), 2):
                pair = cols[i : i + 2]
                x = pair[0][1]
                if len(pair) == 2:
                    x = [jnp.concatenate([u, v], axis=1) for u, v in zip(x, pair[1][1])]
                x = jnp.concatenate(x, axis=0)
                if part == 2:
                    o = jnp.dot(w_ref[:, :640], jnp.concatenate(split(x), axis=0), preferred_element_type=F32)
                else:
                    o = jnp.dot(w_ref[:, 640:], x.astype(BF16), preferred_element_type=F32)
                o = o[:BV] + o[BV:]
                for q, (key, _) in enumerate(pair):
                    out.append((key, o[:, LANES * q : LANES * (q + 1)]))
        return out

    if count <= 4:
        x = {(b, t): value(n.terms, t, buf) for b, n in enumerate(nodes) for t in ring}
        side = {t: (ring[(i + 1) % count], ring[i - 1]) for i, t in enumerate(ring)}
        out = couple(
            lambda b, t: x[b, t],
            lambda b, t: [x[b, u] for u in side[t]],
            [(b, t) for t in ring for b, n in enumerate(nodes) if n.tiles is None or t in n.tiles],
        )
        for (b, t), v in out:
            y = nodes[b].s * (v - d_ref[t] * x[b, t])
            buf[nodes[b].slot, t] = x[b, t] + y if nodes[b].keep else y
        return

    @pl.loop(0, count)
    def _(t):
        for b, n in enumerate(nodes):
            xbuf[b, t] = value(n.terms, t, buf)

    @pl.loop(0, count)
    def _(t):
        sides = (lax.rem(t + 1, count), lax.rem(t + count - 1, count))
        out = couple(
            lambda b, u: xbuf[b, u],
            lambda b, u: [xbuf[b, v] for v in sides],
            [(b, t) for b in range(len(nodes))],
        )
        for (b, _), v in out:
            x = xbuf[b, t]
            y = nodes[b].s * (v - d_ref[t] * x)
            buf[nodes[b].slot, t] = x + y if nodes[b].keep else y


def run(plan, op, buf, xbuf):
    for nodes in plan.levels:
        ring = list(range(plan.count))
        if plan.count <= 4 and all(n.tiles is not None for n in nodes):
            ring = [t for t in ring if t in set().union(*[n.near for n in nodes])]
        run_level(nodes, ring, op, buf, xbuf)


def scratch_for(plan):
    t = plan.count
    return [
        pltpu.VMEM((t, 256, 4 * LANES), BF16),
        pltpu.VMEM((t, 8, LANES), F32),
        pltpu.VMEM((t, BV, LANES), F32),
        pltpu.VMEM((plan.total, t, BV, LANES), F32),
        pltpu.VMEM((plan.width if t > 4 else 1, t if t > 4 else 1, BV, LANES), F32),
    ]


def call(kernel, outs, scratch, args, flops=1):
    specs = [pl.BlockSpec(memory_space=pltpu.VMEM)] * len(args)
    single = not isinstance(outs, (list, tuple))
    shapes = [outs] if single else list(outs)
    res = pl.pallas_call(
        kernel,
        out_shape=shapes,
        in_specs=specs,
        out_specs=[pl.BlockSpec(memory_space=pltpu.VMEM)] * len(shapes),
        scratch_shapes=scratch,
        compiler_params=pltpu.CompilerParams(vmem_limit_bytes=VMEM_LIMIT),
        cost_estimate=pl.CostEstimate(flops=flops, bytes_accessed=1 << 20, transcendentals=0),
    )(*args)
    return res[0] if single else res


def shape(*dims, dtype=F32):
    return jax.ShapeDtypeStruct(dims, dtype)


def pack_kernel(b, w0, blocks, coeffs, damping, neighbors, up, dn, par, wcat):
    lane = lax.broadcasted_iota(jnp.int32, (BV, LANES), 1)
    nb = neighbors[...]
    low = jnp.bitwise_and(nb, LANES - 1)
    tile = lax.shift_right_logical(nb, 7)
    code = jnp.where(tile == lax.axis_index("space"), low, low + LANES).astype(F32)
    p = jnp.concatenate(
        [damping[...], coeffs[...], jnp.zeros((3, LANES), F32), code, jnp.zeros((4, LANES), F32)], axis=0
    )
    par[...] = p
    for ref in (up, dn):
        ref[0:PAR] = p
        ref[PAR : PAR + BV] = w0[...]
    base = PAR + BV
    for i in range(4):
        r = slice(base + BV * i, base + BV * (i + 1))
        up[r] = jnp.where(lane >= 32, b[4 * i], pltpu.roll(b[4 * i + 2], 32, 1))
        dn[r] = jnp.where(lane < 96, b[4 * i], pltpu.roll(b[4 * i + 2], 96, 1))
    for h in range(2):
        r = slice(base + BV * (4 + h), base + BV * (5 + h))
        other = pltpu.roll(b[8 * h + 5], 64, 1)
        up[r] = jnp.where(lane >= 64, b[8 * h + 1], other)
        dn[r] = jnp.where(lane < 64, b[8 * h + 1], other)
    w = jnp.concatenate([blocks[k] for k in range(5)], axis=1)
    hi, lo = split(w)
    hi, lo = hi.astype(F32), lo.astype(F32)
    top = jnp.concatenate([hi, hi, hi], axis=1)
    bot = jnp.concatenate([lo, jnp.zeros_like(w), lo], axis=1)
    wcat[...] = jnp.concatenate([top, bot], axis=0).astype(BF16)


def fine_plan():
    plan = Plan(3)
    bs = [[Input(None) for _ in range(3)] for _ in range(4)]
    w0 = Input(None)
    first = plan.apply(w0, S0)
    outs = []
    for i in range(4):
        f0 = lin((1.0, bs[i][0]), *([(1.0, first)] if i == 0 else []))
        f1 = lin((1.0, plan.apply(f0, S0)), (1.0, bs[i][1]))
        f2 = lin((1.0, plan.apply(f1, S0)), (1.0, bs[i][2]))
        q3 = plan.apply(f2, S0, tiles={0})
        q3.near = {0, 1, 2}
        outs.append((f0, f1, f2, q3))
    plan.schedule([n for o in outs for f in o for _, n in (f if isinstance(f, list) else [(1, f)]) if isinstance(n, Node)])
    return plan, bs, w0, outs


def fine_kernel(b, w0, par, left, right, wcat, g, g_par, late, f, s_ref, cf_ref, d_ref, buf, xbuf):
    plan, bs, w_in, outs = fine_plan()
    src = [par, right, left]
    build_operator(lambda t: src[t][0:PAR], 3, s_ref, cf_ref, d_ref)
    base = PAR + BV

    def get(i, m, t):
        if t == 0:
            return b[4 * i + m]
        ref = (None, right, left)[t]
        if m == 1:
            x = ref[base + BV * (4 + i // 2) : base + BV * (5 + i // 2)]
            return pltpu.roll(x, 64, 1) if i % 2 else x
        x = ref[base + BV * i : base + BV * (i + 1)]
        if m == 0:
            return x
        return pltpu.roll(x, 32 if t == 1 else 96, 1)

    for i in range(4):
        for m in range(3):
            bs[i][m].get = functools.partial(get, i, m)
    on = jnp.where(lax.axis_index("tm") == 0, 1.0, 0.0).astype(F32)
    w_in.get = lambda t: on * (w0[...] if t == 0 else src[t][PAR : PAR + BV])
    run(plan, (s_ref, cf_ref, d_ref, wcat), buf, xbuf)
    for i in range(4):
        f0, f1, f2, q3 = outs[i]
        f[i] = value(f0, 0, buf)
        f[4 + i] = value(f1, 0, buf)
        f[8 + i] = value(f2, 0, buf)
        last = buf[q3.slot, 0] + b[4 * i + 3]
        if i < 3:
            g[BV * i : BV * (i + 1)] = last
            g_par[BV * i : BV * (i + 1)] = last
        if i > 1:
            late[BV * (i - 2) : BV * (i - 1)] = last
    g_par[3 * BV :] = par[...]


def tiles_of(g_refs, prev_refs, par_refs):
    if not par_refs:
        ref, prev = g_refs[0], prev_refs[0]
        return (
            lambda i, t: ref[t, BV * i : BV * (i + 1)],
            lambda i, t: prev[t, BV * i : BV * (i + 1)],
            lambda t: ref[t, 3 * BV :],
        )
    return (
        lambda i, t: g_refs[t][BV * i : BV * (i + 1)],
        lambda i, t: prev_refs[t][BV * i : BV * (i + 1)],
        lambda t: par_refs[t][0:PAR] if t != 2 else g_refs[t][3 * BV :],
    )


def middle_plan(count):
    plan = Plan(count)
    g = [Input(None) for _ in range(5)]
    gm2, gm1, g0, g1, g2 = g
    t = lin((1.0, plan.apply(gm1, S1, 2)), (1.0, g0))
    a = lin((1.0, plan.apply(t, S1, 2)), (1.0, g1))
    k = lin((1.0, plan.apply(a, S1, 2)), (1.0, g2))
    r = lin((2.0, gm1), (-1.0, plan.apply(gm2, S1)))
    p = lin((1.0, plan.apply(r, S1)), (1.0, g0))
    plan.schedule([n for f in (a, k, p) for _, n in f if isinstance(n, Node)])
    return plan, g, (k, p, a)


def each_tile(count, body):
    if count <= 4:
        for t in range(count):
            body(t)
    else:
        pl.loop(0, count)(body)


def middle_kernel(count, n_g, n_par, wcat, *refs):
    g_refs, prev_refs, refs = refs[:n_g], refs[n_g : 2 * n_g], refs[2 * n_g :]
    par_refs, refs = refs[:n_par], refs[n_par:]
    kp, a_out, s_ref, cf_ref, d_ref, buf, xbuf = refs
    plan, g, (k, p, a) = middle_plan(count)
    g_at, prev_at, par_at = tiles_of(g_refs, prev_refs, par_refs)
    build_operator(par_at, count, s_ref, cf_ref, d_ref)
    for i in range(2):
        g[i].get = functools.partial(prev_at, i)
    for i in range(3):
        g[2 + i].get = functools.partial(g_at, i)
    run(plan, (s_ref, cf_ref, d_ref, wcat), buf, xbuf)

    def store(t):
        kp[0, t] = value(k, t, buf)
        kp[1, t] = value(p, t, buf)
        a_out[t] = value(a, t, buf)

    each_tile(count, store)


def final_plan(count, n_tm):
    plan = Plan(count)
    ks = {n: Input(None) for n in range(1, n_tm)}
    ps = {n: Input(None) for n in range(1, n_tm)}
    gm2, gm1, g0, g1, g2, g3 = gs = [Input(None) for _ in range(6)]
    a = Input(None)
    P = lambda x, n=1: plan.power(x, S0, n)
    Q = lambda x, n=1, parts=1: plan.power(x, S1, n, parts)
    R = lambda x, parts=1: plan.apply(x, S2, parts)
    top = n_tm - 1
    delta = {top - 1: lin((1.0, ks[top]))}
    deltap = {}
    pi = lin((1.0, ps[top]))
    for n in range(top - 1, 1, -1):
        if n - 1 > 1:
            if n in deltap:
                deltap[n - 1] = lin((1.0, R(deltap[n])), (1.0, delta[n]))
            else:
                deltap[n - 1] = delta[n]
        delta[n - 1] = lin((1.0, R(delta[n], 2)), (1.0, ks[n]))
        pi = lin((1.0, R(pi)), (1.0, ps[n]))
    q4d = {n: Q(delta[n], 4, 2) for n in (1, 2)}
    theta = {n: lin((1.0, ks[n]), (1.0, q4d[n])) for n in (1, 2)}
    thetap = lin((1.0, delta[2]), (1.0, Q(deltap[2], 4)))
    u = lin((1.0, pi), (4.0, Q(thetap, 2)))
    d2 = lin((1.0, plan.excess(u, S0)), (1.0, P(Q(plan.excess(deltap[3], S1), 6), 4)))
    q2 = Q(theta[2], 2, 2)
    q3 = Q(q2, 1, 2)
    um = lin((1.0, ps[1]), (4.0, q2))
    m = lin((1.0, plan.excess(um, S0)), (1.0, P(Q(plan.excess(delta[3], S1), 6), 4)))
    q4d2 = Q(d2, 4)
    v = lin((1.0, m), (1.0, q4d2))
    v0 = lin((1.0, a), (1.0, q3), (1.0, v))
    h = lin((1.0, plan.excess(lin((1.0, q3), (1.0, a)), S0)), (1.0, plan.excess(q4d[2], S1)), (1.0, Q(v)))
    v1 = lin((1.0, theta[1]), (1.0, h))
    qh = Q(h)
    qt, xt = Q(theta[1], 1, 2), plan.excess(theta[1], S0)
    x0 = plan.excess(gm1, S0)
    e4 = lin((1.0, gm1), (1.0, qt))
    v2 = lin((1.0, e4), (1.0, xt), (1.0, qh))
    e5 = lin((1.0, g0), (1.0, Q(e4, 1, 2)))
    h6 = lin((1.0, x0), (1.0, Q(lin((2.0, xt), (1.0, qh)))))
    v3 = lin((1.0, e5), (1.0, h6))
    x1 = plan.excess(lin((1.0, g0), (1.0, Q(gm1))), S0)
    h7 = lin((1.0, x1), (1.0, Q(lin((1.0, h6), (1.0, Q(xt))))))
    v4 = lin((1.0, g1), (1.0, Q(e5, 1, 2)), (1.0, h7), (-1.0, plan.excess(q4d2, S1)))
    near = {0, 1, count - 1} if count == 4 else None

    def P_near(x, tiles):
        y = plan.apply(x, S0, tiles=tiles)
        if tiles is not None:
            y.near = near
        return y

    own = {0} if near else None
    c2 = []
    for n, x in enumerate((v0, v1, v2, v3, v4)):
        y = lin((1.0, P(x, 4)), (1.0, gs[n]))
        y = P(y, 2)
        y = P_near(P_near(y, near), near)
        c2.append(lin((1.0, y), (1.0, gs[n + 1])))
    hom = []
    for n in range(4):
        y1 = P_near(c2[n], near)
        y2 = P_near(y1, near)
        y3 = P_near(y2, own)
        hom.append((y1, y2, y3))
    finals = [n for y in hom for n in y] + [n for c in c2 for _, n in c if isinstance(n, Node)]
    plan.schedule(finals)
    return plan, ks, ps, gs, a, c2, hom


def final_kernel(count, n_tm, n_g, n_par, aprev, late, f, wcat, *refs):
    blocks, refs = refs[:n_tm], refs[n_tm:]
    g_refs, prev_refs, refs = refs[:n_g], refs[n_g : 2 * n_g], refs[2 * n_g :]
    par_refs, refs = refs[:n_par], refs[n_par:]
    out, kbuf, s_ref, cf_ref, d_ref, buf, xbuf = refs
    plan, ks, ps, gs, a, c2, hom = final_plan(count, n_tm)
    g_at, prev_at, par_at = tiles_of(g_refs, prev_refs, par_refs)
    build_operator(par_at, count, s_ref, cf_ref, d_ref)
    j = lax.axis_index("tm")
    odd = jnp.bitwise_and(j, 1)
    for ref, (even_mask, odd_mask) in zip(blocks, owners()):
        n = j - jnp.bitwise_xor(j, jnp.where(odd == 1, odd_mask, even_mask))

        @pl.when(n >= 1)
        def _(ref=ref, n=n):
            kbuf[n - 1] = ref[...]

    for n in range(1, n_tm):

        @pl.when(n > j)
        def _(n=n):
            kbuf[n - 1] = jnp.zeros(kbuf.shape[1:], F32)

        ks[n].get = functools.partial(lambda n, t: kbuf[n - 1, 0, t], n)
        ps[n].get = functools.partial(lambda n, t: kbuf[n - 1, 1, t], n)
    for i in range(2):
        gs[i].get = functools.partial(prev_at, i)
    for i in range(3):
        gs[2 + i].get = functools.partial(g_at, i)
    gs[5].get = lambda t: late[BV:]
    a.get = lambda t: aprev[t]
    run(plan, (s_ref, cf_ref, d_ref, wcat), buf, xbuf)
    for n in range(4):
        for m in range(3):
            out[4 * n + m] = f[4 * m + n] + buf[hom[n][m].slot, 0]
        out[4 * n + 3] = value(c2[n + 1], 0, buf)


CROSS = ((2, 4), (4, 2), (6, 6))


def owners():
    mine = ((0, 0),) + CROSS
    return mine + tuple((o ^ 1, e ^ 1) for e, o in mine)


def shards(forcing, initial, blocks, coeffs, damping, neighbors):
    n_tm, n_sp = lax.axis_size("tm"), lax.axis_size("space")
    count = n_sp
    sp = lax.axis_index("space")

    def around(x, r):
        return lax.ppermute(x, "space", [((i + r) % n_sp, i) for i in range(n_sp)])

    halo = PAR + BV + 6 * BV
    up, dn, par, wcat = call(
        pack_kernel,
        [shape(halo, LANES), shape(halo, LANES), shape(PAR, LANES), shape(2 * BV, 960, dtype=BF16)],
        [],
        (forcing, initial, blocks, coeffs, damping, neighbors),
    )
    left, right = around(up, -1), around(dn, 1)
    plan = fine_plan()[0]
    g, g_par, late, f = call(
        fine_kernel,
        [shape(3 * BV, LANES), shape(3 * BV + PAR, LANES), shape(2 * BV, LANES), shape(12, BV, LANES)],
        scratch_for(plan),
        (forcing, initial, par, left, right, wcat),
    )
    chain = [(i, i + 1) for i in range(n_tm - 1)]
    prev = lax.ppermute(late, "tm", chain)
    if n_sp == 4:
        gs = [g, around(g, 1), around(g_par, 2), around(g, 3)]
        prevs = [prev] + [around(prev, r) for r in (1, 2, 3)]
        pars = [par, right, par, left]
    else:
        gs, prevs = ([jnp.roll(lax.all_gather(x, "space", axis=0), -sp, axis=0)] for x in (g_par, prev))
        pars = []
    n_g, n_par = len(gs), len(pars)
    plan = middle_plan(count)[0]
    kp, a = call(
        functools.partial(middle_kernel, count, n_g, n_par),
        [shape(2, count, BV, LANES), shape(count, BV, LANES)],
        scratch_for(plan),
        (wcat, *gs, *prevs, *pars),
    )

    def swap(x, even, odd):
        return lax.ppermute(x, "tm", [(i, i ^ (odd if i % 2 else even)) for i in range(n_tm)])

    mine = [kp] + [swap(kp, *m) for m in CROSS]
    aprev = lax.ppermute(a, "tm", chain)
    theirs = [swap(x, 1, 1) for x in mine[:3]]
    last, aprev = lax.optimization_barrier((mine[3], aprev))
    theirs.append(swap(last, 1, 1))
    plan = final_plan(count, n_tm)[0]
    return call(
        functools.partial(final_kernel, count, n_tm, n_g, n_par),
        shape(16, BV, LANES),
        [pltpu.VMEM((n_tm - 1, 2, count, BV, LANES), F32)] + scratch_for(plan),
        (aprev, late, f, wcat, *mine, *theirs, *gs, *prevs, *pars),
    )


def solution(mesh):
    spec = PartitionSpec
    in_specs = (
        spec("tm", None, "space"),
        spec(None, "space"),
        spec(),
        spec(None, "space"),
        spec(None, "space"),
        spec(None, "space"),
    )
    return jax.shard_map(
        shards, mesh=mesh, in_specs=in_specs, out_specs=spec("tm", None, "space"), check_vma=False
    )
```

```python
import functools

import jax
import jax.numpy as jnp
from jax import lax
from jax.experimental import pallas as pl
from jax.experimental.pallas import tpu as pltpu
from jax.sharding import PartitionSpec

F32 = jnp.float32
BF16 = jnp.bfloat16
BV = 64
LANES = 128
S0 = 0.015625
S1 = S0 * 4
S2 = S0 * 16
PAR = 80
FILL = 4
VMEM_LIMIT = 60 * 1024 * 1024


def split(x):
    hi = x.astype(BF16)
    return hi, (x - hi.astype(F32)).astype(BF16)


class Node:
    def __init__(self, plan, terms, s, parts, keep, tiles, near):
        self.terms, self.s, self.parts, self.keep, self.tiles, self.near = terms, s, parts, keep, tiles, near
        self.level = 1 + max([t.level for _, t in terms] + [0])
        self.done = False
        plan.nodes.append(self)
        plan.depth = max(plan.depth, self.level)


class Input:
    level = 0

    def __init__(self, get):
        self.get = get


def lin(*terms):
    flat = []
    for c, v in terms:
        if isinstance(v, list):
            flat += [(c * d, n) for d, n in v]
        else:
            flat.append((c, v))
    merged = []
    for c, v in flat:
        for i, (d, n) in enumerate(merged):
            if n is v:
                merged[i] = (c + d, n)
                break
        else:
            merged.append((c, v))
    return [(c, n) for c, n in merged if c != 0]


class Plan:
    def __init__(self, count):
        self.nodes, self.depth, self.count = [], 0, count

    def apply(self, x, s, parts=1, keep=True, tiles=None, near=None):
        if not isinstance(x, list):
            x = [(1.0, x)]
        return Node(self, x, s, parts, keep, tiles, near)

    def power(self, x, s, n, parts=1):
        for _ in range(n):
            x = self.apply(x, s, parts)
        return x

    def excess(self, x, s, tiles=None, near=None):
        part = lambda y, tiles=near: self.apply(y, s, 1, False, tiles, near)
        y = part(lin((4.0, x), (1.0, part(x))))
        return part(part(lin((6.0, x), (1.0, y))), tiles)

    def schedule(self, finals):
        used = {}
        for n in reversed(self.nodes):
            n.latest = self.depth
            for u in used.get(id(n), []):
                n.latest = min(n.latest, u.latest - 1)
            for _, t in n.terms:
                used.setdefault(id(t), []).append(n)
        final_ids = {id(n) for n in finals}
        todo, self.levels = list(self.nodes), []
        for level in range(1, self.depth + 1):
            ready = [n for n in todo if all(isinstance(t, Input) or t.done for _, t in n.terms)]
            ready.sort(key=lambda n: n.latest)
            now = [n for i, n in enumerate(ready) if n.latest == level or i < FILL]
            for n in now:
                n.level = level
            todo = [n for n in todo if n not in now]
            self.levels.append(now)
            for n in now:
                n.done = True
        free, total = [], 0
        for nodes in self.levels:
            for n in self.nodes:
                if hasattr(n, "slot") and not getattr(n, "freed", False) and id(n) not in final_ids:
                    last = max([u.level for u in used.get(id(n), [])] + [n.level])
                    if last <= nodes[0].level:
                        n.freed = True
                        free.append(n.slot)
            for n in nodes:
                if free:
                    n.slot = free.pop()
                else:
                    n.slot = total
                    total += 1
        self.total = total
        self.width = max(len(l) for l in self.levels)


def build_operator(par_get, count, s_ref, cf_ref, d_ref):
    rows = lax.broadcasted_iota(jnp.int32, (256, LANES), 0)
    for t in range(count):
        par = par_get(t)
        d_ref[t] = par[:BV]
        cf_ref[t] = par[BV : BV + 8]
        for k in range(4):
            code = par[BV + 8 + k : BV + 9 + k].astype(jnp.int32)
            s_ref[t, :, LANES * k : LANES * (k + 1)] = jnp.where(rows == code, 1.0, 0.0).astype(BF16)


def value(terms, t, buf):
    total = None
    for c, v in terms:
        x = buf[v.slot, t] if isinstance(v, Node) else v.get(t)
        x = x if c == 1.0 else c * x
        total = x if total is None else total + x
    return total


def unique(items):
    seen = []
    for t in items:
        if not any(t is u for u in seen):
            seen.append(t)
    return seen


def run_level(nodes, ring, op, buf, xbuf):
    s_ref, cf_ref, d_ref, w_ref = op
    count = len(ring)
    lane = lax.broadcasted_iota(jnp.int32, (BV, LANES), 1)
    parts = [n.parts for n in nodes]

    def couple(at, near, blocks):
        columns = {1: [], 2: []}
        for t in unique(t for _, t in blocks):
            here = [b for b, u in blocks if u is t]
            stack = []
            for b in here:
                right, left = near(b, t)
                x = jnp.concatenate([at(b, t), jnp.where(lane < 64, right, left)], axis=1)
                stack += list(split(x)) if parts[b] == 2 else [x.astype(BF16)]
            got = jnp.dot(jnp.concatenate(stack, axis=0), s_ref[t], preferred_element_type=F32)
            cf, row = cf_ref[t], 0
            for b in here:
                pick = got[row : row + BV]
                if parts[b] == 2:
                    pick = pick + got[row + BV : row + 2 * BV]
                row += BV * parts[b]
                col = [at(b, t) * cf[0:1]]
                col += [pick[:, LANES * k : LANES * (k + 1)] * cf[k + 1 : k + 2] for k in range(4)]
                columns[parts[b]].append(((b, t), col))
        out = []
        for part, cols in columns.items():
            for i in range(0, len(cols), 2):
                pair = cols[i : i + 2]
                x = pair[0][1]
                if len(pair) == 2:
                    x = [jnp.concatenate([u, v], axis=1) for u, v in zip(x, pair[1][1])]
                x = jnp.concatenate(x, axis=0)
                if part == 2:
                    o = jnp.dot(w_ref[:, :640], jnp.concatenate(split(x), axis=0), preferred_element_type=F32)
                else:
                    o = jnp.dot(w_ref[:, 640:], x.astype(BF16), preferred_element_type=F32)
                o = o[:BV] + o[BV:]
                for q, (key, _) in enumerate(pair):
                    out.append((key, o[:, LANES * q : LANES * (q + 1)]))
        return out

    if count <= 4:
        rings = [ring if n.near is None else [t for t in ring if t in n.near] for n in nodes]
        x = {(b, t): value(n.terms, t, buf) for b, n in enumerate(nodes) for t in rings[b]}
        side = [{t: (r[(i + 1) % len(r)], r[i - 1]) for i, t in enumerate(r)} for r in rings]
        out = couple(
            lambda b, t: x[b, t],
            lambda b, t: [x[b, u] for u in side[b][t]],
            [(b, t) for t in ring for b, n in enumerate(nodes) if (t in rings[b] if n.tiles is None else t in n.tiles)],
        )
        for (b, t), v in out:
            y = nodes[b].s * (v - d_ref[t] * x[b, t])
            buf[nodes[b].slot, t] = x[b, t] + y if nodes[b].keep else y
        return

    @pl.loop(0, count)
    def _(t):
        for b, n in enumerate(nodes):
            xbuf[b, t] = value(n.terms, t, buf)

    @pl.loop(0, count)
    def _(t):
        sides = (lax.rem(t + 1, count), lax.rem(t + count - 1, count))
        out = couple(
            lambda b, u: xbuf[b, u],
            lambda b, u: [xbuf[b, v] for v in sides],
            [(b, t) for b in range(len(nodes))],
        )
        for (b, _), v in out:
            x = xbuf[b, t]
            y = nodes[b].s * (v - d_ref[t] * x)
            buf[nodes[b].slot, t] = x + y if nodes[b].keep else y


def run(plan, op, buf, xbuf):
    for nodes in plan.levels:
        run_level(nodes, list(range(plan.count)), op, buf, xbuf)


def scratch_for(plan):
    t = plan.count
    return [
        pltpu.VMEM((t, 256, 4 * LANES), BF16),
        pltpu.VMEM((t, 8, LANES), F32),
        pltpu.VMEM((t, BV, LANES), F32),
        pltpu.VMEM((plan.total, t, BV, LANES), F32),
        pltpu.VMEM((plan.width if t > 4 else 1, t if t > 4 else 1, BV, LANES), F32),
    ]


def call(kernel, outs, scratch, args, flops=1, unplaced=()):
    specs = [pl.BlockSpec(memory_space=pl.ANY if i in unplaced else pltpu.VMEM) for i in range(len(args))]
    single = not isinstance(outs, (list, tuple))
    shapes = [outs] if single else list(outs)
    res = pl.pallas_call(
        kernel,
        out_shape=shapes,
        in_specs=specs,
        out_specs=[pl.BlockSpec(memory_space=pltpu.VMEM)] * len(shapes),
        scratch_shapes=scratch,
        compiler_params=pltpu.CompilerParams(vmem_limit_bytes=VMEM_LIMIT),
        cost_estimate=pl.CostEstimate(flops=flops, bytes_accessed=1 << 20, transcendentals=0),
    )(*args)
    return res[0] if single else res


def shape(*dims, dtype=F32):
    return jax.ShapeDtypeStruct(dims, dtype)


def pack_kernel(b, w0, blocks, coeffs, damping, neighbors, up, dn, par, wcat):
    lane = lax.broadcasted_iota(jnp.int32, (BV, LANES), 1)
    nb = neighbors[...]
    low = jnp.bitwise_and(nb, LANES - 1)
    tile = lax.shift_right_logical(nb, 7)
    code = jnp.where(tile == lax.axis_index("space"), low, low + LANES).astype(F32)
    p = jnp.concatenate(
        [damping[...], coeffs[...], jnp.zeros((3, LANES), F32), code, jnp.zeros((4, LANES), F32)], axis=0
    )
    par[...] = p
    for ref in (up, dn):
        ref[0:PAR] = p
        ref[PAR : PAR + BV] = w0[...]
    base = PAR + BV
    for i in range(4):
        r = slice(base + BV * i, base + BV * (i + 1))
        up[r] = jnp.where(lane >= 32, b[4 * i], pltpu.roll(b[4 * i + 2], 32, 1))
        dn[r] = jnp.where(lane < 96, b[4 * i], pltpu.roll(b[4 * i + 2], 96, 1))
    for h in range(2):
        r = slice(base + BV * (4 + h), base + BV * (5 + h))
        other = pltpu.roll(b[8 * h + 5], 64, 1)
        up[r] = jnp.where(lane >= 64, b[8 * h + 1], other)
        dn[r] = jnp.where(lane < 64, b[8 * h + 1], other)
    w = jnp.concatenate([blocks[k] for k in range(5)], axis=1)
    hi, lo = split(w)
    hi, lo = hi.astype(F32), lo.astype(F32)
    top = jnp.concatenate([hi, hi, hi], axis=1)
    bot = jnp.concatenate([lo, jnp.zeros_like(w), lo], axis=1)
    wcat[...] = jnp.concatenate([top, bot], axis=0).astype(BF16)


def fine_plan():
    plan = Plan(3)
    bs = [[Input(None) for _ in range(3)] for _ in range(4)]
    w0 = Input(None)
    first = plan.apply(w0, S0)
    outs = []
    for i in range(4):
        f0 = lin((1.0, bs[i][0]), *([(1.0, first)] if i == 0 else []))
        f1 = lin((1.0, plan.apply(f0, S0)), (1.0, bs[i][1]))
        f2 = lin((1.0, plan.apply(f1, S0)), (1.0, bs[i][2]))
        q3 = plan.apply(f2, S0, tiles={0})
        outs.append((f0, f1, f2, q3))
    plan.schedule([n for o in outs for f in o for _, n in (f if isinstance(f, list) else [(1, f)]) if isinstance(n, Node)])
    return plan, bs, w0, outs


def fine_kernel(b, w0, par, left, right, wcat, g, g_par, late, f, s_ref, cf_ref, d_ref, buf, xbuf):
    plan, bs, w_in, outs = fine_plan()
    src = [par, right, left]
    build_operator(lambda t: src[t][0:PAR], 3, s_ref, cf_ref, d_ref)
    base = PAR + BV

    def get(i, m, t):
        if t == 0:
            return b[4 * i + m]
        ref = (None, right, left)[t]
        if m == 1:
            x = ref[base + BV * (4 + i // 2) : base + BV * (5 + i // 2)]
            return pltpu.roll(x, 64, 1) if i % 2 else x
        x = ref[base + BV * i : base + BV * (i + 1)]
        if m == 0:
            return x
        return pltpu.roll(x, 32 if t == 1 else 96, 1)

    for i in range(4):
        for m in range(3):
            bs[i][m].get = functools.partial(get, i, m)
    on = jnp.where(lax.axis_index("tm") == 0, 1.0, 0.0).astype(F32)
    w_in.get = lambda t: on * (w0[...] if t == 0 else src[t][PAR : PAR + BV])
    run(plan, (s_ref, cf_ref, d_ref, wcat), buf, xbuf)
    for i in range(4):
        f0, f1, f2, q3 = outs[i]
        f[i] = value(f0, 0, buf)
        f[4 + i] = value(f1, 0, buf)
        f[8 + i] = value(f2, 0, buf)
        last = buf[q3.slot, 0] + b[4 * i + 3]
        if i < 3:
            g[BV * i : BV * (i + 1)] = last
            g_par[BV * i : BV * (i + 1)] = last
        if i > 1:
            late[BV * (i - 2) : BV * (i - 1)] = last
    g_par[3 * BV :] = par[...]


def tiles_of(g_refs, prev_refs, par_refs):
    if not par_refs:
        ref, prev = g_refs[0], prev_refs[0]
        return (
            lambda i, t: ref[t, BV * i : BV * (i + 1)],
            lambda i, t: prev[t, BV * i : BV * (i + 1)],
            lambda t: ref[t, 3 * BV :],
        )
    return (
        lambda i, t: g_refs[t][BV * i : BV * (i + 1)],
        lambda i, t: prev_refs[t][BV * i : BV * (i + 1)],
        lambda t: par_refs[t][0:PAR] if t != 2 else g_refs[t][3 * BV :],
    )


def middle_plan(count):
    plan = Plan(count)
    g = [Input(None) for _ in range(5)]
    gm2, gm1, g0, g1, g2 = g
    t = lin((1.0, plan.apply(gm1, S1, 2)), (1.0, g0))
    a = lin((1.0, plan.apply(t, S1, 2)), (1.0, g1))
    k = lin((1.0, plan.apply(a, S1, 2)), (1.0, g2))
    r = lin((2.0, gm1), (-1.0, plan.apply(gm2, S1)))
    p = lin((1.0, plan.apply(r, S1)), (1.0, g0))
    k, p, a = (plan.power(x, S0, 8) for x in (k, p, a))
    plan.schedule([k, p, a])
    return plan, g, (k, p, a)


def each_tile(count, body):
    if count <= 4:
        for t in range(count):
            body(t)
    else:
        pl.loop(0, count)(body)


def middle_kernel(count, n_g, n_par, wcat, *refs):
    g_refs, prev_refs, refs = refs[:n_g], refs[n_g : 2 * n_g], refs[2 * n_g :]
    par_refs, refs = refs[:n_par], refs[n_par:]
    kp, a_out, s_ref, cf_ref, d_ref, buf, xbuf = refs
    plan, g, (k, p, a) = middle_plan(count)
    g_at, prev_at, par_at = tiles_of(g_refs, prev_refs, par_refs)
    build_operator(par_at, count, s_ref, cf_ref, d_ref)
    for i in range(2):
        g[i].get = functools.partial(prev_at, i)
    for i in range(3):
        g[2 + i].get = functools.partial(g_at, i)
    run(plan, (s_ref, cf_ref, d_ref, wcat), buf, xbuf)

    def store(t):
        kp[0, t] = buf[k.slot, t]
        kp[1, t] = buf[p.slot, t]
        a_out[t] = buf[a.slot, t]

    each_tile(count, store)


def local_plan(count):
    plan = Plan(count)
    gm2, gm1, g0, g1, g2, g3 = gs = [Input(None) for _ in range(6)]
    P = lambda x, n: plan.power(x, S0, n)
    Q = lambda x: plan.apply(x, S1, 2)
    near = {0, 1, count - 1} if count == 4 else None
    t = lin((1.0, g0), (1.0, Q(gm1)))
    w3 = lin((1.0, t), (1.0, plan.excess(gm1, S0)))
    w4 = lin((1.0, g1), (1.0, Q(w3)), (1.0, plan.excess(t, S0)))
    w2 = P(gm1, 4)
    outs = []
    for n, w in enumerate((None, None, w2, P(w3, 4), P(w4, 4))):
        x = lin((1.0, gs[n]), *([] if w is None else [(1.0, w)]))
        y = plan.apply(P(x, 2), S0, tiles=near)
        outs.append(lin((1.0, gs[n + 1]), (1.0, plan.apply(y, S0, tiles=near, near=near))))
    plan.schedule([n for o in outs for _, n in o if isinstance(n, Node)])
    return plan, gs, outs


def local_kernel(count, n_g, n_par, late, wcat, *refs):
    g_refs, prev_refs, refs = refs[:n_g], refs[n_g : 2 * n_g], refs[2 * n_g :]
    par_refs, refs = refs[:n_par], refs[n_par:]
    out, s_ref, cf_ref, d_ref, buf, xbuf = refs
    plan, gs, outs = local_plan(count)
    g_at, prev_at, par_at = tiles_of(g_refs, prev_refs, par_refs)
    build_operator(par_at, count, s_ref, cf_ref, d_ref)
    for i in range(2):
        gs[i].get = functools.partial(prev_at, i)
    for i in range(3):
        gs[2 + i].get = functools.partial(g_at, i)
    gs[5].get = lambda t: late[BV:]
    run(plan, (s_ref, cf_ref, d_ref, wcat), buf, xbuf)

    def store(t):
        for n in range(5):
            out[n, t] = value(outs[n], t, buf) if count != 4 or t != 2 else jnp.zeros((BV, LANES), F32)

    each_tile(count, store)


def final_plan(count, n_tm):
    plan = Plan(count)
    ks = {n: Input(None) for n in range(1, n_tm)}
    ps = {n: Input(None) for n in range(1, n_tm)}
    locals_in = [Input(None) for _ in range(5)]
    a = Input(None)
    P = lambda x, n=1: plan.power(x, S0, n)
    Q = lambda x, n=1, parts=1: plan.power(x, S1, n, parts)
    R = lambda x, parts=1: plan.apply(x, S2, parts)
    top = n_tm - 1
    delta = {top - 1: lin((1.0, ks[top]))}
    deltap = {}
    pi = lin((1.0, ps[top]))
    for n in range(top - 1, 1, -1):
        if n - 1 > 1:
            if n in deltap:
                deltap[n - 1] = lin((1.0, R(deltap[n])), (1.0, delta[n]))
            else:
                deltap[n - 1] = delta[n]
        delta[n - 1] = lin((1.0, R(delta[n], 2)), (1.0, ks[n]))
        pi = lin((1.0, R(pi)), (1.0, ps[n]))
    q4d = {n: Q(delta[n], 4, 2) for n in (1, 2)}
    theta = {n: lin((1.0, ks[n]), (1.0, q4d[n])) for n in (1, 2)}
    thetap = lin((1.0, delta[2]), (1.0, Q(deltap[2], 4)))
    u = lin((1.0, pi), (4.0, Q(thetap, 2)))
    d2 = lin((1.0, plan.excess(u, S0)), (1.0, P(Q(plan.excess(deltap[3], S1), 6), 4)))
    q2 = Q(theta[2], 2, 2)
    q3 = Q(q2, 1, 2)
    um = lin((1.0, ps[1]), (4.0, q2))
    m = lin((1.0, plan.excess(um, S0)), (1.0, P(Q(plan.excess(delta[3], S1), 6), 4)))
    q4d2 = Q(d2, 4)
    v = lin((1.0, m), (1.0, q4d2))
    v0 = lin((1.0, a), (1.0, q3), (1.0, v))
    h = lin((1.0, plan.excess(lin((1.0, q3), (1.0, a)), S0)), (1.0, plan.excess(q4d[2], S1)), (1.0, Q(v)))
    v1 = lin((1.0, theta[1]), (1.0, h))
    qh = Q(h)
    qt, xt = Q(theta[1], 1, 2), plan.excess(theta[1], S0)
    v2 = lin((1.0, qt), (1.0, xt), (1.0, qh))
    v3 = Q(lin((1.0, v2), (1.0, xt)), 1, 2)
    near = {0, 1, count - 1} if count == 4 else None
    own = {0} if near else None
    v4 = lin(
        (1.0, plan.apply(lin((1.0, v3), (1.0, Q(xt))), S1, 2, tiles=own, near=near)),
        (-1.0, plan.excess(q4d2, S1, own, near)),
    )
    c2 = [lin((1.0, v), (1.0, x)) for v, x in zip((v0, v1, v2, v3, v4), locals_in)]
    hom = []
    for n in range(4):
        y1 = plan.apply(c2[n], S0, 2, tiles=near, near=near)
        y2 = plan.apply(y1, S0, 2, tiles=near, near=near)
        y3 = plan.apply(y2, S0, 2, tiles=own, near=near)
        hom.append((y1, y2, y3))
    finals = [n for y in hom for n in y] + [n for c in c2 for _, n in c if isinstance(n, Node)]
    plan.schedule(finals)
    return plan, ks, ps, locals_in, a, c2, hom


def final_kernel(count, n_tm, aprev, near_part, f, wcat, *refs):
    blocks, refs = refs[:n_tm], refs[n_tm:]
    par_refs = refs[:-8]
    out, kbuf, sems, s_ref, cf_ref, d_ref, buf, xbuf = refs[-8:]
    plan, ks, ps, locals_in, a, c2, hom = final_plan(count, n_tm)
    par_at = tiles_of(par_refs, par_refs, par_refs if len(par_refs) > 1 else ())[2]
    j = lax.axis_index("tm")
    odd = jnp.bitwise_and(j, 1)
    fetches = []
    for i, (ref, (even_mask, odd_mask)) in enumerate(zip(blocks, owners())):
        n = j - jnp.bitwise_xor(j, jnp.where(odd == 1, odd_mask, even_mask))
        fetches.append((n, pltpu.make_async_copy(ref, kbuf.at[jnp.maximum(n - 1, 0)], sems.at[i])))
    for n, copy in fetches:
        pl.when(n >= 1)(copy.start)
    build_operator(par_at, count, s_ref, cf_ref, d_ref)
    for n in range(1, n_tm):

        @pl.when(n > j)
        def _(n=n):
            kbuf[n - 1] = jnp.zeros(kbuf.shape[1:], F32)

        ks[n].get = functools.partial(lambda n, t: kbuf[n - 1, 0, t], n)
        ps[n].get = functools.partial(lambda n, t: kbuf[n - 1, 1, t], n)
    for n, x in enumerate(locals_in):
        x.get = functools.partial(lambda n, t: near_part[n, t], n)
    for n, copy in fetches:
        pl.when(n >= 1)(copy.wait)
    a.get = lambda t: aprev[t]
    run(plan, (s_ref, cf_ref, d_ref, wcat), buf, xbuf)
    for n in range(4):
        for m in range(3):
            out[4 * n + m] = f[4 * m + n] + buf[hom[n][m].slot, 0]
        out[4 * n + 3] = value(c2[n + 1], 0, buf)


CROSS = ((2, 4), (4, 2), (6, 6))


def owners():
    mine = ((0, 0),) + CROSS
    return mine + tuple((o ^ 1, e ^ 1) for e, o in mine)


def shards(forcing, initial, blocks, coeffs, damping, neighbors):
    n_tm, n_sp = lax.axis_size("tm"), lax.axis_size("space")
    count = n_sp
    sp = lax.axis_index("space")

    def around(x, r):
        return lax.ppermute(x, "space", [((i + r) % n_sp, i) for i in range(n_sp)])

    halo = PAR + BV + 6 * BV
    up, dn, par, wcat = call(
        pack_kernel,
        [shape(halo, LANES), shape(halo, LANES), shape(PAR, LANES), shape(2 * BV, 960, dtype=BF16)],
        [],
        (forcing, initial, blocks, coeffs, damping, neighbors),
    )
    left, right = around(up, -1), around(dn, 1)
    plan = fine_plan()[0]
    g, g_par, late, f = call(
        fine_kernel,
        [shape(3 * BV, LANES), shape(3 * BV + PAR, LANES), shape(2 * BV, LANES), shape(12, BV, LANES)],
        scratch_for(plan),
        (forcing, initial, par, left, right, wcat),
    )
    chain = [(i, i + 1) for i in range(n_tm - 1)]
    prev = lax.ppermute(late, "tm", chain)
    if n_sp == 4:
        gs = [g, around(g, 1), around(g_par, 2), around(g, 3)]
        prevs = [prev] + [around(prev, r) for r in (1, 2, 3)]
        pars = [par, right, par, left]
    else:
        gs, prevs = ([jnp.roll(lax.all_gather(x, "space", axis=0), -sp, axis=0)] for x in (g_par, prev))
        pars = []
    n_g, n_par = len(gs), len(pars)
    plan = middle_plan(count)[0]
    kp, a = call(
        functools.partial(middle_kernel, count, n_g, n_par),
        [shape(2, count, BV, LANES), shape(count, BV, LANES)],
        scratch_for(plan),
        (wcat, *gs, *prevs, *pars),
    )

    def swap(x, even, odd):
        return lax.ppermute(x, "tm", [(i, i ^ (odd if i % 2 else even)) for i in range(n_tm)])

    mine = [kp] + [swap(kp, *m) for m in CROSS]
    aprev = lax.ppermute(a, "tm", chain)
    plan = local_plan(count)[0]
    late, aprev, _ = lax.optimization_barrier((late, aprev, kp))
    near_part = call(
        functools.partial(local_kernel, count, n_g, n_par),
        shape(5, count, BV, LANES),
        scratch_for(plan),
        (late, wcat, *gs, *prevs, *pars),
        flops=8 << 30,
    )
    *mine, near_part = lax.optimization_barrier((*mine, near_part))
    theirs = [swap(x, 1, 1) for x in mine]
    plan = final_plan(count, n_tm)[0]
    return call(
        functools.partial(final_kernel, count, n_tm),
        shape(16, BV, LANES),
        [pltpu.VMEM((n_tm - 1, 2, count, BV, LANES), F32), pltpu.SemaphoreType.DMA((n_tm,))] + scratch_for(plan),
        (aprev, near_part, f, wcat, *mine, *theirs, *((par, right, gs[2], left) if n_sp == 4 else gs)),
        unplaced=range(4, 4 + n_tm),
    )


def solution(mesh):
    spec = PartitionSpec
    in_specs = (
        spec("tm", None, "space"),
        spec(None, "space"),
        spec(),
        spec(None, "space"),
        spec(None, "space"),
        spec(None, "space"),
    )
    return jax.shard_map(
        shards, mesh=mesh, in_specs=in_specs, out_specs=spec("tm", None, "space"), check_vma=False
    )
```

```python
import functools

import jax
import jax.numpy as jnp
from jax import lax
from jax.experimental import pallas as pl
from jax.experimental.pallas import tpu as pltpu
from jax.sharding import PartitionSpec

F32 = jnp.float32
BF16 = jnp.bfloat16
BV = 64
LANES = 128
S0 = 0.015625
S1 = S0 * 4
S2 = S0 * 16
PAR = 80
FILL = 4
VMEM_LIMIT = 60 * 1024 * 1024


def split(x):
    hi = x.astype(BF16)
    return hi, (x - hi.astype(F32)).astype(BF16)


class Node:
    def __init__(self, plan, terms, s, parts, keep, tiles, near):
        self.terms, self.s, self.parts, self.keep, self.tiles, self.near = terms, s, parts, keep, tiles, near
        self.level = 1 + max([t.level for _, t in terms] + [0])
        self.done = False
        plan.nodes.append(self)
        plan.depth = max(plan.depth, self.level)


class Input:
    level = 0

    def __init__(self, get):
        self.get = get


def lin(*terms):
    flat = []
    for c, v in terms:
        if isinstance(v, list):
            flat += [(c * d, n) for d, n in v]
        else:
            flat.append((c, v))
    merged = []
    for c, v in flat:
        for i, (d, n) in enumerate(merged):
            if n is v:
                merged[i] = (c + d, n)
                break
        else:
            merged.append((c, v))
    return [(c, n) for c, n in merged if c != 0]


class Plan:
    def __init__(self, count):
        self.nodes, self.depth, self.count = [], 0, count

    def apply(self, x, s, parts=1, keep=True, tiles=None, near=None):
        if not isinstance(x, list):
            x = [(1.0, x)]
        return Node(self, x, s, parts, keep, tiles, near)

    def power(self, x, s, n, parts=1):
        for _ in range(n):
            x = self.apply(x, s, parts)
        return x

    def excess(self, x, s, tiles=None, near=None):
        part = lambda y, tiles=near: self.apply(y, s, 1, False, tiles, near)
        y = part(lin((4.0, x), (1.0, part(x))))
        return part(part(lin((6.0, x), (1.0, y))), tiles)

    def schedule(self, finals):
        used = {}
        for n in reversed(self.nodes):
            n.latest = self.depth
            for u in used.get(id(n), []):
                n.latest = min(n.latest, u.latest - 1)
            for _, t in n.terms:
                used.setdefault(id(t), []).append(n)
        final_ids = {id(n) for n in finals}
        todo, self.levels = list(self.nodes), []
        for level in range(1, self.depth + 1):
            ready = [n for n in todo if all(isinstance(t, Input) or t.done for _, t in n.terms)]
            ready.sort(key=lambda n: n.latest)
            now = [n for i, n in enumerate(ready) if n.latest == level or i < FILL]
            for n in now:
                n.level = level
            todo = [n for n in todo if n not in now]
            self.levels.append(now)
            for n in now:
                n.done = True
        free, total = [], 0
        for nodes in self.levels:
            for n in self.nodes:
                if hasattr(n, "slot") and not getattr(n, "freed", False) and id(n) not in final_ids:
                    last = max([u.level for u in used.get(id(n), [])] + [n.level])
                    if last <= nodes[0].level:
                        n.freed = True
                        free.append(n.slot)
            for n in nodes:
                if free:
                    n.slot = free.pop()
                else:
                    n.slot = total
                    total += 1
        self.total = total
        self.width = max(len(l) for l in self.levels)


def build_operator(par_get, count, s_ref, cf_ref, d_ref):
    rows = lax.broadcasted_iota(jnp.int32, (256, LANES), 0)
    for t in range(count):
        par = par_get(t)
        d_ref[t] = par[:BV]
        cf_ref[t] = par[BV : BV + 8]
        for k in range(4):
            code = par[BV + 8 + k : BV + 9 + k].astype(jnp.int32)
            s_ref[t, :, LANES * k : LANES * (k + 1)] = jnp.where(rows == code, 1.0, 0.0).astype(BF16)


def value(terms, t, buf):
    total = None
    for c, v in terms:
        x = buf[v.slot, t] if isinstance(v, Node) else v.get(t)
        x = x if c == 1.0 else c * x
        total = x if total is None else total + x
    return total


def unique(items):
    seen = []
    for t in items:
        if not any(t is u for u in seen):
            seen.append(t)
    return seen


def run_level(nodes, ring, op, buf, xbuf):
    s_ref, cf_ref, d_ref, w_ref = op
    count = len(ring)
    lane = lax.broadcasted_iota(jnp.int32, (BV, LANES), 1)
    parts = [n.parts for n in nodes]

    def couple(at, near, blocks):
        columns = {1: [], 2: []}
        for t in unique(t for _, t in blocks):
            here = [b for b, u in blocks if u is t]
            stack = []
            for b in here:
                right, left = near(b, t)
                x = jnp.concatenate([at(b, t), jnp.where(lane < 64, right, left)], axis=1)
                stack += list(split(x)) if parts[b] == 2 else [x.astype(BF16)]
            got = jnp.dot(jnp.concatenate(stack, axis=0), s_ref[t], preferred_element_type=F32)
            cf, row = cf_ref[t], 0
            for b in here:
                pick = got[row : row + BV]
                if parts[b] == 2:
                    pick = pick + got[row + BV : row + 2 * BV]
                row += BV * parts[b]
                col = [at(b, t) * cf[0:1]]
                col += [pick[:, LANES * k : LANES * (k + 1)] * cf[k + 1 : k + 2] for k in range(4)]
                columns[parts[b]].append(((b, t), col))
        out = []
        for part, cols in columns.items():
            for i in range(0, len(cols), 2):
                pair = cols[i : i + 2]
                x = pair[0][1]
                if len(pair) == 2:
                    x = [jnp.concatenate([u, v], axis=1) for u, v in zip(x, pair[1][1])]
                x = jnp.concatenate(x, axis=0)
                if part == 2:
                    o = jnp.dot(w_ref[:, :640], jnp.concatenate(split(x), axis=0), preferred_element_type=F32)
                else:
                    o = jnp.dot(w_ref[:, 640:], x.astype(BF16), preferred_element_type=F32)
                o = o[:BV] + o[BV:]
                for q, (key, _) in enumerate(pair):
                    out.append((key, o[:, LANES * q : LANES * (q + 1)]))
        return out

    if count <= 4:
        rings = [ring if n.near is None else [t for t in ring if t in n.near] for n in nodes]
        x = {(b, t): value(n.terms, t, buf) for b, n in enumerate(nodes) for t in rings[b]}
        side = [{t: (r[(i + 1) % len(r)], r[i - 1]) for i, t in enumerate(r)} for r in rings]
        out = couple(
            lambda b, t: x[b, t],
            lambda b, t: [x[b, u] for u in side[b][t]],
            [(b, t) for t in ring for b, n in enumerate(nodes) if (t in rings[b] if n.tiles is None else t in n.tiles)],
        )
        for (b, t), v in out:
            y = nodes[b].s * (v - d_ref[t] * x[b, t])
            buf[nodes[b].slot, t] = x[b, t] + y if nodes[b].keep else y
        return

    @pl.loop(0, count)
    def _(t):
        for b, n in enumerate(nodes):
            xbuf[b, t] = value(n.terms, t, buf)

    @pl.loop(0, count)
    def _(t):
        sides = (lax.rem(t + 1, count), lax.rem(t + count - 1, count))
        out = couple(
            lambda b, u: xbuf[b, u],
            lambda b, u: [xbuf[b, v] for v in sides],
            [(b, t) for b in range(len(nodes))],
        )
        for (b, _), v in out:
            x = xbuf[b, t]
            y = nodes[b].s * (v - d_ref[t] * x)
            buf[nodes[b].slot, t] = x + y if nodes[b].keep else y


def run(plan, op, buf, xbuf):
    for nodes in plan.levels:
        run_level(nodes, list(range(plan.count)), op, buf, xbuf)


def scratch_for(plan):
    t = plan.count
    return [
        pltpu.VMEM((t, 256, 4 * LANES), BF16),
        pltpu.VMEM((t, 8, LANES), F32),
        pltpu.VMEM((t, BV, LANES), F32),
        pltpu.VMEM((plan.total, t, BV, LANES), F32),
        pltpu.VMEM((plan.width if t > 4 else 1, t if t > 4 else 1, BV, LANES), F32),
    ]


def call(kernel, outs, scratch, args, flops=1, unplaced=()):
    specs = [pl.BlockSpec(memory_space=pl.ANY if i in unplaced else pltpu.VMEM) for i in range(len(args))]
    single = not isinstance(outs, (list, tuple))
    shapes = [outs] if single else list(outs)
    res = pl.pallas_call(
        kernel,
        out_shape=shapes,
        in_specs=specs,
        out_specs=[pl.BlockSpec(memory_space=pltpu.VMEM)] * len(shapes),
        scratch_shapes=scratch,
        compiler_params=pltpu.CompilerParams(vmem_limit_bytes=VMEM_LIMIT),
        cost_estimate=pl.CostEstimate(flops=flops, bytes_accessed=1 << 20, transcendentals=0),
    )(*args)
    return res[0] if single else res


def shape(*dims, dtype=F32):
    return jax.ShapeDtypeStruct(dims, dtype)


def pack_kernel(b, w0, blocks, coeffs, damping, neighbors, up, dn, par, wcat):
    lane = lax.broadcasted_iota(jnp.int32, (BV, LANES), 1)
    nb = neighbors[...]
    low = jnp.bitwise_and(nb, LANES - 1)
    tile = lax.shift_right_logical(nb, 7)
    code = jnp.where(tile == lax.axis_index("space"), low, low + LANES).astype(F32)
    p = jnp.concatenate(
        [damping[...], coeffs[...], jnp.zeros((3, LANES), F32), code, jnp.zeros((4, LANES), F32)], axis=0
    )
    par[...] = p
    for ref in (up, dn):
        ref[0:PAR] = p
        ref[PAR : PAR + BV] = w0[...]
    base = PAR + BV
    for i in range(4):
        r = slice(base + BV * i, base + BV * (i + 1))
        up[r] = jnp.where(lane >= 32, b[4 * i], pltpu.roll(b[4 * i + 2], 32, 1))
        dn[r] = jnp.where(lane < 96, b[4 * i], pltpu.roll(b[4 * i + 2], 96, 1))
    for h in range(2):
        r = slice(base + BV * (4 + h), base + BV * (5 + h))
        other = pltpu.roll(b[8 * h + 5], 64, 1)
        up[r] = jnp.where(lane >= 64, b[8 * h + 1], other)
        dn[r] = jnp.where(lane < 64, b[8 * h + 1], other)
    w = jnp.concatenate([blocks[k] for k in range(5)], axis=1)
    hi, lo = split(w)
    hi, lo = hi.astype(F32), lo.astype(F32)
    top = jnp.concatenate([hi, hi, hi], axis=1)
    bot = jnp.concatenate([lo, jnp.zeros_like(w), lo], axis=1)
    wcat[...] = jnp.concatenate([top, bot], axis=0).astype(BF16)


def fine_plan():
    plan = Plan(3)
    bs = [[Input(None) for _ in range(3)] for _ in range(4)]
    w0 = Input(None)
    first = plan.apply(w0, S0)
    outs = []
    for i in range(4):
        f0 = lin((1.0, bs[i][0]), *([(1.0, first)] if i == 0 else []))
        f1 = lin((1.0, plan.apply(f0, S0)), (1.0, bs[i][1]))
        f2 = lin((1.0, plan.apply(f1, S0)), (1.0, bs[i][2]))
        q3 = plan.apply(f2, S0, tiles={0})
        outs.append((f0, f1, f2, q3))
    plan.schedule([n for o in outs for f in o for _, n in (f if isinstance(f, list) else [(1, f)]) if isinstance(n, Node)])
    return plan, bs, w0, outs


def fine_kernel(b, w0, par, left, right, wcat, g, g_par, late, f, s_ref, cf_ref, d_ref, buf, xbuf):
    plan, bs, w_in, outs = fine_plan()
    src = [par, right, left]
    build_operator(lambda t: src[t][0:PAR], 3, s_ref, cf_ref, d_ref)
    base = PAR + BV

    def get(i, m, t):
        if t == 0:
            return b[4 * i + m]
        ref = (None, right, left)[t]
        if m == 1:
            x = ref[base + BV * (4 + i // 2) : base + BV * (5 + i // 2)]
            return pltpu.roll(x, 64, 1) if i % 2 else x
        x = ref[base + BV * i : base + BV * (i + 1)]
        if m == 0:
            return x
        return pltpu.roll(x, 32 if t == 1 else 96, 1)

    for i in range(4):
        for m in range(3):
            bs[i][m].get = functools.partial(get, i, m)
    on = jnp.where(lax.axis_index("tm") == 0, 1.0, 0.0).astype(F32)
    w_in.get = lambda t: on * (w0[...] if t == 0 else src[t][PAR : PAR + BV])
    run(plan, (s_ref, cf_ref, d_ref, wcat), buf, xbuf)
    for i in range(4):
        f0, f1, f2, q3 = outs[i]
        f[i] = value(f0, 0, buf)
        f[4 + i] = value(f1, 0, buf)
        f[8 + i] = value(f2, 0, buf)
        last = buf[q3.slot, 0] + b[4 * i + 3]
        if i < 3:
            g[BV * i : BV * (i + 1)] = last
            g_par[BV * i : BV * (i + 1)] = last
        if i > 1:
            late[BV * (i - 2) : BV * (i - 1)] = last
    g_par[3 * BV :] = par[...]


def tiles_of(g_refs, prev_refs, par_refs):
    if not par_refs:
        ref, prev = g_refs[0], prev_refs[0]
        return (
            lambda i, t: ref[t, BV * i : BV * (i + 1)],
            lambda i, t: prev[t, BV * i : BV * (i + 1)],
            lambda t: ref[t, 3 * BV :],
        )
    return (
        lambda i, t: g_refs[t][BV * i : BV * (i + 1)],
        lambda i, t: prev_refs[t][BV * i : BV * (i + 1)],
        lambda t: par_refs[t][0:PAR] if t != 2 else g_refs[t][3 * BV :],
    )


def middle_plan(count):
    plan = Plan(count)
    g = [Input(None) for _ in range(5)]
    gm2, gm1, g0, g1, g2 = g
    t = lin((1.0, plan.apply(gm1, S1, 2)), (1.0, g0))
    a = lin((1.0, plan.apply(t, S1, 2)), (1.0, g1))
    k = lin((1.0, plan.apply(a, S1, 2)), (1.0, g2))
    r = lin((2.0, gm1), (-1.0, plan.apply(gm2, S1)))
    p = lin((1.0, plan.apply(r, S1)), (1.0, g0))
    k, p = (plan.power(x, S0, 4) for x in (k, p))
    plan.schedule([k, p] + [n for _, n in a if isinstance(n, Node)])
    return plan, g, (k, p, a)


def each_tile(count, body):
    if count <= 4:
        for t in range(count):
            body(t)
    else:
        pl.loop(0, count)(body)


def middle_kernel(count, n_g, n_par, wcat, *refs):
    g_refs, prev_refs, refs = refs[:n_g], refs[n_g : 2 * n_g], refs[2 * n_g :]
    par_refs, refs = refs[:n_par], refs[n_par:]
    kp, a_out, s_ref, cf_ref, d_ref, buf, xbuf = refs
    plan, g, (k, p, a) = middle_plan(count)
    g_at, prev_at, par_at = tiles_of(g_refs, prev_refs, par_refs)
    build_operator(par_at, count, s_ref, cf_ref, d_ref)
    for i in range(2):
        g[i].get = functools.partial(prev_at, i)
    for i in range(3):
        g[2 + i].get = functools.partial(g_at, i)
    run(plan, (s_ref, cf_ref, d_ref, wcat), buf, xbuf)

    def store(t):
        kp[0, t] = buf[k.slot, t]
        kp[1, t] = buf[p.slot, t]
        a_out[t] = value(a, t, buf)

    each_tile(count, store)


def local_plan(count):
    plan = Plan(count)
    gm2, gm1, g0, g1, g2 = gs = [Input(None) for _ in range(5)]
    a = Input(None)
    P = lambda x, n: plan.power(x, S0, n)
    Q = lambda x: plan.apply(x, S1, 2)
    t = lin((1.0, g0), (1.0, Q(gm1)))
    w3 = lin((1.0, t), (1.0, plan.excess(gm1, S0)))
    w4 = lin((1.0, g1), (1.0, Q(w3)), (1.0, plan.excess(t, S0)))
    outs = [lin((1.0, gs[n]), (1.0, P(w, 4))) for n, w in ((2, gm1), (3, w3), (4, w4))]
    outs.append([(1.0, P(a, 4))])
    plan.schedule([n for o in outs for _, n in o if isinstance(n, Node)])
    return plan, gs, a, outs


def local_kernel(count, n_g, n_par, aprev, wcat, *refs):
    g_refs, prev_refs, refs = refs[:n_g], refs[n_g : 2 * n_g], refs[2 * n_g :]
    par_refs, refs = refs[:n_par], refs[n_par:]
    out, s_ref, cf_ref, d_ref, buf, xbuf = refs
    plan, gs, a, outs = local_plan(count)
    a.get = lambda t: aprev[t]
    g_at, prev_at, par_at = tiles_of(g_refs, prev_refs, par_refs)
    build_operator(par_at, count, s_ref, cf_ref, d_ref)
    for i in range(2):
        gs[i].get = functools.partial(prev_at, i)
    for i in range(3):
        gs[2 + i].get = functools.partial(g_at, i)
    run(plan, (s_ref, cf_ref, d_ref, wcat), buf, xbuf)

    def store(t):
        for n in range(4):
            out[n, t] = value(outs[n], t, buf)

    each_tile(count, store)


def final_plan(count, n_tm):
    plan = Plan(count)
    ks = {n: Input(None) for n in range(1, n_tm)}
    ps = {n: Input(None) for n in range(1, n_tm)}
    locals_in = [Input(None) for _ in range(3)]
    gs = [Input(None) for _ in range(6)]
    a = Input(None)
    P = lambda x, n=1: plan.power(x, S0, n)
    Q = lambda x, n=1, parts=1: plan.power(x, S1, n, parts)
    R = lambda x, parts=1: plan.apply(x, S2, parts)
    top = n_tm - 1
    delta = {top - 1: lin((1.0, ks[top]))}
    deltap = {}
    pi = lin((1.0, ps[top]))
    for n in range(top - 1, 1, -1):
        if n - 1 > 1:
            if n in deltap:
                deltap[n - 1] = lin((1.0, R(deltap[n])), (1.0, delta[n]))
            else:
                deltap[n - 1] = delta[n]
        delta[n - 1] = lin((1.0, R(delta[n], 2)), (1.0, ks[n]))
        pi = lin((1.0, R(pi)), (1.0, ps[n]))
    q4d = {n: Q(delta[n], 4, 2) for n in (1, 2)}
    theta = {n: lin((1.0, ks[n]), (1.0, q4d[n])) for n in (1, 2)}
    thetap = lin((1.0, delta[2]), (1.0, Q(deltap[2], 4)))
    u = lin((1.0, pi), (4.0, Q(thetap, 2)))
    d2 = lin((1.0, plan.excess(u, S0)), (1.0, P(Q(plan.excess(deltap[3], S1), 6), 4)))
    q2 = Q(theta[2], 2, 2)
    q3 = Q(q2, 1, 2)
    um = lin((1.0, ps[1]), (4.0, q2))
    m = lin((1.0, plan.excess(um, S0)), (1.0, P(Q(plan.excess(delta[3], S1), 6), 4)))
    q4d2 = Q(d2, 4)
    v = lin((1.0, m), (1.0, q4d2))
    v0 = lin((1.0, a), (1.0, q3), (1.0, v))
    h = lin((1.0, plan.excess(lin((1.0, q3), (1.0, a)), S0)), (1.0, plan.excess(q4d[2], S1)), (1.0, Q(v)))
    v1 = lin((1.0, theta[1]), (1.0, h))
    qh = Q(h)
    qt, xt = Q(theta[1], 1, 2), plan.excess(theta[1], S0)
    v2 = lin((1.0, qt), (1.0, xt), (1.0, qh))
    v3 = Q(lin((1.0, v2), (1.0, xt)), 1, 2)
    near = {0, 1, count - 1} if count == 4 else None
    own = {0} if near else None
    v4 = lin((1.0, Q(lin((1.0, v3), (1.0, Q(xt))), 1, 2)), (-1.0, plan.excess(q4d2, S1)))
    near_P = lambda x, tiles: plan.apply(x, S0, tiles=tiles, near=near)
    c2 = []
    for n, (v, x) in enumerate(zip((v0, v1, v2, v3, v4), gs[:2] + locals_in)):
        y = P(lin((1.0, v), (1.0, x)), 2) if n < 4 else near_P(near_P(lin((1.0, v), (1.0, x)), near), near)
        y = near_P(plan.apply(y, S0, tiles=near, near=near if n == 4 else None), near if n < 4 else own)
        c2.append(lin((1.0, y), (1.0, gs[n + 1])))
    hom = []
    for n in range(4):
        y1 = plan.apply(c2[n], S0, tiles=near, near=near)
        y2 = plan.apply(y1, S0, tiles=near, near=near)
        y3 = plan.apply(y2, S0, tiles=own, near=near)
        hom.append((y1, y2, y3))
    finals = [n for y in hom for n in y] + [n for c in c2 for _, n in c if isinstance(n, Node)]
    plan.schedule(finals)
    return plan, ks, ps, gs, locals_in, a, c2, hom


def final_kernel(count, n_tm, n_g, n_par, near_part, late, f, wcat, *refs):
    blocks, refs = refs[:n_tm], refs[n_tm:]
    g_refs, prev_refs, refs = refs[:n_g], refs[n_g : 2 * n_g], refs[2 * n_g :]
    par_refs, refs = refs[:n_par], refs[n_par:]
    out, kbuf, sems, s_ref, cf_ref, d_ref, buf, xbuf = refs
    plan, ks, ps, gs, locals_in, a, c2, hom = final_plan(count, n_tm)
    g_at, prev_at, par_at = tiles_of(g_refs, prev_refs, par_refs)
    j = lax.axis_index("tm")
    odd = jnp.bitwise_and(j, 1)
    fetches = []
    for i, (ref, (even_mask, odd_mask)) in enumerate(zip(blocks, owners())):
        n = j - jnp.bitwise_xor(j, jnp.where(odd == 1, odd_mask, even_mask))
        fetches.append((n, pltpu.make_async_copy(ref, kbuf.at[jnp.maximum(n - 1, 0)], sems.at[i])))
    for n, copy in fetches:
        pl.when(n >= 1)(copy.start)
    build_operator(par_at, count, s_ref, cf_ref, d_ref)
    for n in range(1, n_tm):

        @pl.when(n > j)
        def _(n=n):
            kbuf[n - 1] = jnp.zeros(kbuf.shape[1:], F32)

        ks[n].get = functools.partial(lambda n, t: kbuf[n - 1, 0, t], n)
        ps[n].get = functools.partial(lambda n, t: kbuf[n - 1, 1, t], n)
    for i in range(2):
        gs[i].get = functools.partial(prev_at, i)
    for i in range(3):
        gs[2 + i].get = functools.partial(g_at, i)
    gs[5].get = lambda t: late[BV:]
    for n, x in enumerate(locals_in):
        x.get = functools.partial(lambda n, t: near_part[n, t], n)
    for n, copy in fetches:
        pl.when(n >= 1)(copy.wait)
    a.get = lambda t: near_part[3, t]
    run(plan, (s_ref, cf_ref, d_ref, wcat), buf, xbuf)
    for n in range(4):
        for m in range(3):
            out[4 * n + m] = f[4 * m + n] + buf[hom[n][m].slot, 0]
        out[4 * n + 3] = value(c2[n + 1], 0, buf)


CROSS = ((2, 4), (4, 2), (6, 6))


def owners():
    mine = ((0, 0),) + CROSS
    return mine + tuple((o ^ 1, e ^ 1) for e, o in mine)


def shards(forcing, initial, blocks, coeffs, damping, neighbors):
    n_tm, n_sp = lax.axis_size("tm"), lax.axis_size("space")
    count = n_sp
    sp = lax.axis_index("space")

    def around(x, r):
        return lax.ppermute(x, "space", [((i + r) % n_sp, i) for i in range(n_sp)])

    halo = PAR + BV + 6 * BV
    up, dn, par, wcat = call(
        pack_kernel,
        [shape(halo, LANES), shape(halo, LANES), shape(PAR, LANES), shape(2 * BV, 960, dtype=BF16)],
        [],
        (forcing, initial, blocks, coeffs, damping, neighbors),
    )
    left, right = around(up, -1), around(dn, 1)
    plan = fine_plan()[0]
    g, g_par, late, f = call(
        fine_kernel,
        [shape(3 * BV, LANES), shape(3 * BV + PAR, LANES), shape(2 * BV, LANES), shape(12, BV, LANES)],
        scratch_for(plan),
        (forcing, initial, par, left, right, wcat),
    )
    chain = [(i, i + 1) for i in range(n_tm - 1)]
    prev = lax.ppermute(late, "tm", chain)
    if n_sp == 4:
        gs = [g, around(g, 1), around(g_par, 2), around(g, 3)]
        prevs = [prev] + [around(prev, r) for r in (1, 2, 3)]
        pars = [par, right, par, left]
    else:
        gs, prevs = ([jnp.roll(lax.all_gather(x, "space", axis=0), -sp, axis=0)] for x in (g_par, prev))
        pars = []
    n_g, n_par = len(gs), len(pars)
    plan = middle_plan(count)[0]
    kp, a = call(
        functools.partial(middle_kernel, count, n_g, n_par),
        [shape(2, count, BV, LANES), shape(count, BV, LANES)],
        scratch_for(plan),
        (wcat, *gs, *prevs, *pars),
    )

    def swap(x, even, odd):
        return lax.ppermute(x, "tm", [(i, i ^ (odd if i % 2 else even)) for i in range(n_tm)])

    mine = [kp] + [swap(kp, *m) for m in CROSS]
    aprev = lax.ppermute(a, "tm", chain)
    plan = local_plan(count)[0]
    w_late, _ = lax.optimization_barrier((wcat, kp))
    near_part = call(
        functools.partial(local_kernel, count, n_g, n_par),
        shape(4, count, BV, LANES),
        scratch_for(plan),
        (aprev, w_late, *gs, *prevs, *pars),
        flops=5 << 30,
    )
    theirs = [swap(lax.optimization_barrier((x, near_part))[0], 1, 1) for x in mine]
    plan = final_plan(count, n_tm)[0]
    return call(
        functools.partial(final_kernel, count, n_tm, n_g, n_par),
        shape(16, BV, LANES),
        [pltpu.VMEM((n_tm - 1, 2, count, BV, LANES), F32), pltpu.SemaphoreType.DMA((n_tm,))] + scratch_for(plan),
        (near_part, late, f, wcat, *mine, *theirs, *gs, *prevs, *pars),
        unplaced=range(4, 4 + n_tm),
    )


def solution(mesh):
    spec = PartitionSpec
    in_specs = (
        spec("tm", None, "space"),
        spec(None, "space"),
        spec(),
        spec(None, "space"),
        spec(None, "space"),
        spec(None, "space"),
    )
    return jax.shard_map(
        shards, mesh=mesh, in_specs=in_specs, out_specs=spec("tm", None, "space"), check_vma=False
    )
```

```python
import functools

import jax
import jax.numpy as jnp
from jax import lax
from jax.experimental import pallas as pl
from jax.experimental.pallas import tpu as pltpu
from jax.sharding import PartitionSpec

F32 = jnp.float32
BF16 = jnp.bfloat16
BV = 64
LANES = 128
S0 = 0.015625
S1 = S0 * 4
S2 = S0 * 16
PAR = 80
FILL = 4
VMEM_LIMIT = 60 * 1024 * 1024


def split(x):
    hi = x.astype(BF16)
    return hi, (x - hi.astype(F32)).astype(BF16)


class Node:
    def __init__(self, plan, terms, s, parts, keep, tiles, near):
        self.terms, self.s, self.parts, self.keep, self.tiles, self.near = terms, s, parts, keep, tiles, near
        self.level = 1 + max([t.level for _, t in terms] + [0])
        self.done = False
        plan.nodes.append(self)
        plan.depth = max(plan.depth, self.level)


class Input:
    level = 0

    def __init__(self, get):
        self.get = get


def lin(*terms):
    flat = []
    for c, v in terms:
        if isinstance(v, list):
            flat += [(c * d, n) for d, n in v]
        else:
            flat.append((c, v))
    merged = []
    for c, v in flat:
        for i, (d, n) in enumerate(merged):
            if n is v:
                merged[i] = (c + d, n)
                break
        else:
            merged.append((c, v))
    return [(c, n) for c, n in merged if c != 0]


class Plan:
    def __init__(self, count):
        self.nodes, self.depth, self.count = [], 0, count

    def apply(self, x, s, parts=1, keep=True, tiles=None, near=None):
        if not isinstance(x, list):
            x = [(1.0, x)]
        return Node(self, x, s, parts, keep, tiles, near)

    def power(self, x, s, n, parts=1):
        for _ in range(n):
            x = self.apply(x, s, parts)
        return x

    def excess(self, x, s, tiles=None, near=None):
        part = lambda y, tiles=near: self.apply(y, s, 1, False, tiles, near)
        y = part(lin((4.0, x), (1.0, part(x))))
        return part(part(lin((6.0, x), (1.0, y))), tiles)

    def schedule(self, finals):
        used = {}
        for n in reversed(self.nodes):
            n.latest = self.depth
            for u in used.get(id(n), []):
                n.latest = min(n.latest, u.latest - 1)
            for _, t in n.terms:
                used.setdefault(id(t), []).append(n)
        final_ids = {id(n) for n in finals}
        todo, self.levels = list(self.nodes), []
        for level in range(1, self.depth + 1):
            ready = [n for n in todo if all(isinstance(t, Input) or t.done for _, t in n.terms)]
            ready.sort(key=lambda n: n.latest)
            now = [n for i, n in enumerate(ready) if n.latest == level or i < FILL]
            for n in now:
                n.level = level
            todo = [n for n in todo if n not in now]
            self.levels.append(now)
            for n in now:
                n.done = True
        free, total = [], 0
        for nodes in self.levels:
            for n in self.nodes:
                if hasattr(n, "slot") and not getattr(n, "freed", False) and id(n) not in final_ids:
                    last = max([u.level for u in used.get(id(n), [])] + [n.level])
                    if last <= nodes[0].level:
                        n.freed = True
                        free.append(n.slot)
            for n in nodes:
                if free:
                    n.slot = free.pop()
                else:
                    n.slot = total
                    total += 1
        self.total = total
        self.width = max(len(l) for l in self.levels)


def build_operator(par_get, count, s_ref, cf_ref, d_ref):
    rows = lax.broadcasted_iota(jnp.int32, (256, LANES), 0)
    for t in range(count):
        par = par_get(t)
        d_ref[t] = par[:BV]
        cf_ref[t] = par[BV : BV + 8]
        for k in range(4):
            code = par[BV + 8 + k : BV + 9 + k].astype(jnp.int32)
            s_ref[t, :, LANES * k : LANES * (k + 1)] = jnp.where(rows == code, 1.0, 0.0).astype(BF16)


def value(terms, t, buf):
    total = None
    for c, v in terms:
        x = buf[v.slot, t] if isinstance(v, Node) else v.get(t)
        x = x if c == 1.0 else c * x
        total = x if total is None else total + x
    return total


def unique(items):
    seen = []
    for t in items:
        if not any(t is u for u in seen):
            seen.append(t)
    return seen


def run_level(nodes, ring, op, buf, xbuf):
    s_ref, cf_ref, d_ref, w_ref = op
    count = len(ring)
    lane = lax.broadcasted_iota(jnp.int32, (BV, LANES), 1)
    parts = [n.parts for n in nodes]

    def couple(at, near, blocks):
        columns = {1: [], 2: []}
        for t in unique(t for _, t in blocks):
            here = [b for b, u in blocks if u is t]
            stack = []
            for b in here:
                right, left = near(b, t)
                x = jnp.concatenate([at(b, t), jnp.where(lane < 64, right, left)], axis=1)
                stack += list(split(x)) if parts[b] == 2 else [x.astype(BF16)]
            got = jnp.dot(jnp.concatenate(stack, axis=0), s_ref[t], preferred_element_type=F32)
            cf, row = cf_ref[t], 0
            for b in here:
                pick = got[row : row + BV]
                if parts[b] == 2:
                    pick = pick + got[row + BV : row + 2 * BV]
                row += BV * parts[b]
                col = [at(b, t) * cf[0:1]]
                col += [pick[:, LANES * k : LANES * (k + 1)] * cf[k + 1 : k + 2] for k in range(4)]
                columns[parts[b]].append(((b, t), col))
        out = []
        for part, cols in columns.items():
            for i in range(0, len(cols), 2):
                pair = cols[i : i + 2]
                x = pair[0][1]
                if len(pair) == 2:
                    x = [jnp.concatenate([u, v], axis=1) for u, v in zip(x, pair[1][1])]
                x = jnp.concatenate(x, axis=0)
                if part == 2:
                    o = jnp.dot(w_ref[:, :640], jnp.concatenate(split(x), axis=0), preferred_element_type=F32)
                else:
                    o = jnp.dot(w_ref[:, 640:], x.astype(BF16), preferred_element_type=F32)
                o = o[:BV] + o[BV:]
                for q, (key, _) in enumerate(pair):
                    out.append((key, o[:, LANES * q : LANES * (q + 1)]))
        return out

    if count <= 4:
        rings = [ring if n.near is None else [t for t in ring if t in n.near] for n in nodes]
        x = {(b, t): value(n.terms, t, buf) for b, n in enumerate(nodes) for t in rings[b]}
        side = [{t: (r[(i + 1) % len(r)], r[i - 1]) for i, t in enumerate(r)} for r in rings]
        out = couple(
            lambda b, t: x[b, t],
            lambda b, t: [x[b, u] for u in side[b][t]],
            [(b, t) for t in ring for b, n in enumerate(nodes) if (t in rings[b] if n.tiles is None else t in n.tiles)],
        )
        for (b, t), v in out:
            y = nodes[b].s * (v - d_ref[t] * x[b, t])
            buf[nodes[b].slot, t] = x[b, t] + y if nodes[b].keep else y
        return

    @pl.loop(0, count)
    def _(t):
        for b, n in enumerate(nodes):
            xbuf[b, t] = value(n.terms, t, buf)

    @pl.loop(0, count)
    def _(t):
        sides = (lax.rem(t + 1, count), lax.rem(t + count - 1, count))
        out = couple(
            lambda b, u: xbuf[b, u],
            lambda b, u: [xbuf[b, v] for v in sides],
            [(b, t) for b in range(len(nodes))],
        )
        for (b, _), v in out:
            x = xbuf[b, t]
            y = nodes[b].s * (v - d_ref[t] * x)
            buf[nodes[b].slot, t] = x + y if nodes[b].keep else y


def run(plan, op, buf, xbuf):
    for nodes in plan.levels:
        run_level(nodes, list(range(plan.count)), op, buf, xbuf)


def scratch_for(plan):
    t = plan.count
    return [
        pltpu.VMEM((t, 256, 4 * LANES), BF16),
        pltpu.VMEM((t, 8, LANES), F32),
        pltpu.VMEM((t, BV, LANES), F32),
        pltpu.VMEM((plan.total, t, BV, LANES), F32),
        pltpu.VMEM((plan.width if t > 4 else 1, t if t > 4 else 1, BV, LANES), F32),
    ]


def call(kernel, outs, scratch, args, flops=1, unplaced=()):
    specs = [pl.BlockSpec(memory_space=pl.ANY if i in unplaced else pltpu.VMEM) for i in range(len(args))]
    single = not isinstance(outs, (list, tuple))
    shapes = [outs] if single else list(outs)
    res = pl.pallas_call(
        kernel,
        out_shape=shapes,
        in_specs=specs,
        out_specs=[pl.BlockSpec(memory_space=pltpu.VMEM)] * len(shapes),
        scratch_shapes=scratch,
        compiler_params=pltpu.CompilerParams(vmem_limit_bytes=VMEM_LIMIT),
        cost_estimate=pl.CostEstimate(flops=flops, bytes_accessed=1 << 20, transcendentals=0),
    )(*args)
    return res[0] if single else res


def shape(*dims, dtype=F32):
    return jax.ShapeDtypeStruct(dims, dtype)


def pack_kernel(b, w0, blocks, coeffs, damping, neighbors, up, dn, par, wcat):
    lane = lax.broadcasted_iota(jnp.int32, (BV, LANES), 1)
    nb = neighbors[...]
    low = jnp.bitwise_and(nb, LANES - 1)
    tile = lax.shift_right_logical(nb, 7)
    code = jnp.where(tile == lax.axis_index("space"), low, low + LANES).astype(F32)
    p = jnp.concatenate(
        [damping[...], coeffs[...], jnp.zeros((3, LANES), F32), code, jnp.zeros((4, LANES), F32)], axis=0
    )
    par[...] = p
    for ref in (up, dn):
        ref[0:PAR] = p
        ref[PAR : PAR + BV] = w0[...]
    base = PAR + BV
    for i in range(4):
        r = slice(base + BV * i, base + BV * (i + 1))
        up[r] = jnp.where(lane >= 32, b[4 * i], pltpu.roll(b[4 * i + 2], 32, 1))
        dn[r] = jnp.where(lane < 96, b[4 * i], pltpu.roll(b[4 * i + 2], 96, 1))
    for h in range(2):
        r = slice(base + BV * (4 + h), base + BV * (5 + h))
        other = pltpu.roll(b[8 * h + 5], 64, 1)
        up[r] = jnp.where(lane >= 64, b[8 * h + 1], other)
        dn[r] = jnp.where(lane < 64, b[8 * h + 1], other)
    w = jnp.concatenate([blocks[k] for k in range(5)], axis=1)
    hi, lo = split(w)
    hi, lo = hi.astype(F32), lo.astype(F32)
    top = jnp.concatenate([hi, hi, hi], axis=1)
    bot = jnp.concatenate([lo, jnp.zeros_like(w), lo], axis=1)
    wcat[...] = jnp.concatenate([top, bot], axis=0).astype(BF16)


def fine_plan():
    plan = Plan(3)
    bs = [[Input(None) for _ in range(3)] for _ in range(4)]
    w0 = Input(None)
    first = plan.apply(w0, S0)
    outs = []
    for i in range(4):
        f0 = lin((1.0, bs[i][0]), *([(1.0, first)] if i == 0 else []))
        f1 = lin((1.0, plan.apply(f0, S0)), (1.0, bs[i][1]))
        f2 = lin((1.0, plan.apply(f1, S0)), (1.0, bs[i][2]))
        q3 = plan.apply(f2, S0, tiles={0})
        outs.append((f0, f1, f2, q3))
    plan.schedule([n for o in outs for f in o for _, n in (f if isinstance(f, list) else [(1, f)]) if isinstance(n, Node)])
    return plan, bs, w0, outs


def fine_kernel(b, w0, par, left, right, wcat, g, g_par, late, f, s_ref, cf_ref, d_ref, buf, xbuf):
    plan, bs, w_in, outs = fine_plan()
    src = [par, right, left]
    build_operator(lambda t: src[t][0:PAR], 3, s_ref, cf_ref, d_ref)
    base = PAR + BV

    def get(i, m, t):
        if t == 0:
            return b[4 * i + m]
        ref = (None, right, left)[t]
        if m == 1:
            x = ref[base + BV * (4 + i // 2) : base + BV * (5 + i // 2)]
            return pltpu.roll(x, 64, 1) if i % 2 else x
        x = ref[base + BV * i : base + BV * (i + 1)]
        if m == 0:
            return x
        return pltpu.roll(x, 32 if t == 1 else 96, 1)

    for i in range(4):
        for m in range(3):
            bs[i][m].get = functools.partial(get, i, m)
    on = jnp.where(lax.axis_index("tm") == 0, 1.0, 0.0).astype(F32)
    w_in.get = lambda t: on * (w0[...] if t == 0 else src[t][PAR : PAR + BV])
    run(plan, (s_ref, cf_ref, d_ref, wcat), buf, xbuf)
    for i in range(4):
        f0, f1, f2, q3 = outs[i]
        f[i] = value(f0, 0, buf)
        f[4 + i] = value(f1, 0, buf)
        f[8 + i] = value(f2, 0, buf)
        last = buf[q3.slot, 0] + b[4 * i + 3]
        if i < 3:
            g[BV * i : BV * (i + 1)] = last
            g_par[BV * i : BV * (i + 1)] = last
        if i > 1:
            late[BV * (i - 2) : BV * (i - 1)] = last
    g_par[3 * BV :] = par[...]


def tiles_of(g_refs, prev_refs, par_refs):
    if not par_refs:
        ref, prev = g_refs[0], prev_refs[0]
        return (
            lambda i, t: ref[t, BV * i : BV * (i + 1)],
            lambda i, t: prev[t, BV * i : BV * (i + 1)],
            lambda t: ref[t, 3 * BV :],
        )
    return (
        lambda i, t: g_refs[t][BV * i : BV * (i + 1)],
        lambda i, t: prev_refs[t][BV * i : BV * (i + 1)],
        lambda t: par_refs[t][0:PAR] if t != 2 else g_refs[t][3 * BV :],
    )


def middle_plan(count):
    plan = Plan(count)
    g = [Input(None) for _ in range(5)]
    gm2, gm1, g0, g1, g2 = g
    t = lin((1.0, plan.apply(gm1, S1, 2)), (1.0, g0))
    a = lin((1.0, plan.apply(t, S1, 2)), (1.0, g1))
    k = lin((1.0, plan.apply(a, S1, 2)), (1.0, g2))
    r = lin((2.0, gm1), (-1.0, plan.apply(gm2, S1)))
    p = lin((1.0, plan.apply(r, S1)), (1.0, g0))
    k, p = (plan.power(x, S0, 4) for x in (k, p))
    plan.schedule([k, p] + [n for _, n in a if isinstance(n, Node)])
    return plan, g, (k, p, a)


def each_tile(count, body):
    if count <= 4:
        for t in range(count):
            body(t)
    else:
        pl.loop(0, count)(body)


def middle_kernel(count, n_g, n_par, wcat, *refs):
    g_refs, prev_refs, refs = refs[:n_g], refs[n_g : 2 * n_g], refs[2 * n_g :]
    par_refs, refs = refs[:n_par], refs[n_par:]
    kp, a_out, s_ref, cf_ref, d_ref, buf, xbuf = refs
    plan, g, (k, p, a) = middle_plan(count)
    g_at, prev_at, par_at = tiles_of(g_refs, prev_refs, par_refs)
    build_operator(par_at, count, s_ref, cf_ref, d_ref)
    for i in range(2):
        g[i].get = functools.partial(prev_at, i)
    for i in range(3):
        g[2 + i].get = functools.partial(g_at, i)
    run(plan, (s_ref, cf_ref, d_ref, wcat), buf, xbuf)

    def store(t):
        kp[0, t] = buf[k.slot, t]
        kp[1, t] = buf[p.slot, t]
        a_out[t] = value(a, t, buf)

    each_tile(count, store)


def local_plan(count):
    plan = Plan(count)
    gm2, gm1, g0, g1, g2 = gs = [Input(None) for _ in range(5)]
    a = Input(None)
    P = lambda x, n: plan.power(x, S0, n)
    Q = lambda x: plan.apply(x, S1, 2)
    t = lin((1.0, g0), (1.0, Q(gm1)))
    w3 = lin((1.0, t), (1.0, plan.excess(gm1, S0)))
    w4 = lin((1.0, g1), (1.0, Q(w3)), (1.0, plan.excess(t, S0)))
    outs = [lin((1.0, gs[n]), (1.0, P(w, 4))) for n, w in ((2, gm1), (3, w3), (4, w4))]
    outs.append([(1.0, P(a, 4))])
    plan.schedule([n for o in outs for _, n in o if isinstance(n, Node)])
    return plan, gs, a, outs


def local_kernel(count, n_g, n_par, aprev, wcat, *refs):
    g_refs, prev_refs, refs = refs[:n_g], refs[n_g : 2 * n_g], refs[2 * n_g :]
    par_refs, refs = refs[:n_par], refs[n_par:]
    out, s_ref, cf_ref, d_ref, buf, xbuf = refs
    plan, gs, a, outs = local_plan(count)
    a.get = lambda t: aprev[t]
    g_at, prev_at, par_at = tiles_of(g_refs, prev_refs, par_refs)
    build_operator(par_at, count, s_ref, cf_ref, d_ref)
    for i in range(2):
        gs[i].get = functools.partial(prev_at, i)
    for i in range(3):
        gs[2 + i].get = functools.partial(g_at, i)
    run(plan, (s_ref, cf_ref, d_ref, wcat), buf, xbuf)

    def store(t):
        for n in range(4):
            out[n, t] = value(outs[n], t, buf)

    each_tile(count, store)


def final_plan(count, n_tm):
    plan = Plan(count)
    ks = {n: Input(None) for n in range(1, n_tm)}
    ps = {n: Input(None) for n in range(1, n_tm)}
    locals_in = [Input(None) for _ in range(3)]
    gs = [Input(None) for _ in range(6)]
    a = Input(None)
    P = lambda x, n=1: plan.power(x, S0, n)
    Q = lambda x, n=1, parts=1: plan.power(x, S1, n, parts)
    R = lambda x, parts=1: plan.apply(x, S2, parts)
    top = n_tm - 1
    delta = {top - 1: lin((1.0, ks[top]))}
    deltap = {}
    pi = lin((1.0, ps[top]))
    for n in range(top - 1, 1, -1):
        if n - 1 > 1:
            if n in deltap:
                deltap[n - 1] = lin((1.0, R(deltap[n])), (1.0, delta[n]))
            else:
                deltap[n - 1] = delta[n]
        delta[n - 1] = lin((1.0, R(delta[n], 2)), (1.0, ks[n]))
        pi = lin((1.0, R(pi)), (1.0, ps[n]))
    q4d = {n: Q(delta[n], 4, 2) for n in (1, 2)}
    theta = {n: lin((1.0, ks[n]), (1.0, q4d[n])) for n in (1, 2)}
    thetap = lin((1.0, delta[2]), (1.0, Q(deltap[2], 4)))
    u = lin((1.0, pi), (4.0, Q(thetap, 2)))
    d2 = lin((1.0, plan.excess(u, S0)), (1.0, P(Q(plan.excess(deltap[3], S1), 6), 4)))
    q2 = Q(theta[2], 2, 2)
    q3 = Q(q2, 1, 2)
    um = lin((1.0, ps[1]), (4.0, q2))
    m = lin((1.0, plan.excess(um, S0)), (1.0, P(Q(plan.excess(delta[3], S1), 6), 4)))
    q4d2 = Q(d2, 4)
    v = lin((1.0, m), (1.0, q4d2))
    v0 = lin((1.0, a), (1.0, q3), (1.0, v))
    h = lin((1.0, plan.excess(lin((1.0, q3), (1.0, a)), S0)), (1.0, plan.excess(q4d[2], S1)), (1.0, Q(v)))
    v1 = lin((1.0, theta[1]), (1.0, h))
    qh = Q(h)
    qt, xt = Q(theta[1], 1, 2), plan.excess(theta[1], S0)
    v2 = lin((1.0, qt), (1.0, xt), (1.0, qh))
    v3 = Q(lin((1.0, v2), (1.0, xt)), 1, 2)
    near = {0, 1, count - 1} if count == 4 else None
    own = {0} if near else None
    v4 = lin((1.0, Q(lin((1.0, v3), (1.0, Q(xt))), 1, 2)), (-1.0, plan.excess(q4d2, S1)))
    near_P = lambda x, tiles: plan.apply(x, S0, tiles=tiles, near=near)
    c2 = []
    for n, (v, x) in enumerate(zip((v0, v1, v2, v3, v4), gs[:2] + locals_in)):
        y = P(lin((1.0, v), (1.0, x)), 2) if n < 4 else near_P(near_P(lin((1.0, v), (1.0, x)), near), near)
        y = near_P(plan.apply(y, S0, tiles=near, near=near if n == 4 else None), near if n < 4 else own)
        c2.append(lin((1.0, y), (1.0, gs[n + 1])))
    hom = []
    for n in range(4):
        y1 = plan.apply(c2[n], S0, tiles=near, near=near)
        y2 = plan.apply(y1, S0, tiles=near, near=near)
        y3 = plan.apply(y2, S0, tiles=own, near=near)
        hom.append((y1, y2, y3))
    finals = [n for y in hom for n in y] + [n for c in c2 for _, n in c if isinstance(n, Node)]
    plan.schedule(finals)
    return plan, ks, ps, gs, locals_in, a, c2, hom


def final_kernel(count, n_tm, n_g, n_par, near_part, late, f, wcat, *refs):
    blocks, refs = refs[:n_tm], refs[n_tm:]
    g_refs, prev_refs, refs = refs[:n_g], refs[n_g : 2 * n_g], refs[2 * n_g :]
    par_refs, refs = refs[:n_par], refs[n_par:]
    out, kbuf, sems, s_ref, cf_ref, d_ref, buf, xbuf = refs
    plan, ks, ps, gs, locals_in, a, c2, hom = final_plan(count, n_tm)
    g_at, prev_at, par_at = tiles_of(g_refs, prev_refs, par_refs)
    j = lax.axis_index("tm")
    odd = jnp.bitwise_and(j, 1)
    fetches = []
    for i, (ref, (even_mask, odd_mask)) in enumerate(zip(blocks, owners())):
        n = j - jnp.bitwise_xor(j, jnp.where(odd == 1, odd_mask, even_mask))
        fetches.append((n, pltpu.make_async_copy(ref, kbuf.at[jnp.maximum(n - 1, 0)], sems.at[i])))
    for n, copy in fetches:
        pl.when(n >= 1)(copy.start)
    build_operator(par_at, count, s_ref, cf_ref, d_ref)
    for n in range(1, n_tm):

        @pl.when(n > j)
        def _(n=n):
            kbuf[n - 1] = jnp.zeros(kbuf.shape[1:], F32)

        ks[n].get = functools.partial(lambda n, t: kbuf[n - 1, 0, t], n)
        ps[n].get = functools.partial(lambda n, t: kbuf[n - 1, 1, t], n)
    for i in range(2):
        gs[i].get = functools.partial(prev_at, i)
    for i in range(3):
        gs[2 + i].get = functools.partial(g_at, i)
    gs[5].get = lambda t: late[BV:]
    for n, x in enumerate(locals_in):
        x.get = functools.partial(lambda n, t: near_part[n, t], n)
    for n, copy in fetches:
        pl.when(n >= 1)(copy.wait)
    a.get = lambda t: near_part[3, t]
    run(plan, (s_ref, cf_ref, d_ref, wcat), buf, xbuf)
    for n in range(4):
        for m in range(3):
            out[4 * n + m] = f[4 * m + n] + buf[hom[n][m].slot, 0]
        out[4 * n + 3] = value(c2[n + 1], 0, buf)


CROSS = ((2, 4), (4, 2), (6, 6))


def owners():
    mine = ((0, 0),) + CROSS
    return mine + tuple((o ^ 1, e ^ 1) for e, o in mine)


def shards(forcing, initial, blocks, coeffs, damping, neighbors):
    n_tm, n_sp = lax.axis_size("tm"), lax.axis_size("space")
    count = n_sp
    sp = lax.axis_index("space")

    def around(x, r):
        return lax.ppermute(x, "space", [((i + r) % n_sp, i) for i in range(n_sp)])

    halo = PAR + BV + 6 * BV
    up, dn, par, wcat = call(
        pack_kernel,
        [shape(halo, LANES), shape(halo, LANES), shape(PAR, LANES), shape(2 * BV, 960, dtype=BF16)],
        [],
        (forcing, initial, blocks, coeffs, damping, neighbors),
    )
    left, right = around(up, -1), around(dn, 1)
    plan = fine_plan()[0]
    g, g_par, late, f = call(
        fine_kernel,
        [shape(3 * BV, LANES), shape(3 * BV + PAR, LANES), shape(2 * BV, LANES), shape(12, BV, LANES)],
        scratch_for(plan),
        (forcing, initial, par, left, right, wcat),
    )
    chain = [(i, i + 1) for i in range(n_tm - 1)]
    prev = lax.ppermute(late, "tm", chain)
    if n_sp == 4:
        gs = [g, around(g, 1), around(g_par, 2), around(g, 3)]
        prevs = [prev] + [around(prev, r) for r in (1, 2, 3)]
        pars = [par, right, par, left]
    else:
        gs, prevs = ([jnp.roll(lax.all_gather(x, "space", axis=0), -sp, axis=0)] for x in (g_par, prev))
        pars = []
    n_g, n_par = len(gs), len(pars)
    plan = middle_plan(count)[0]
    kp, a = call(
        functools.partial(middle_kernel, count, n_g, n_par),
        [shape(2, count, BV, LANES), shape(count, BV, LANES)],
        scratch_for(plan),
        (wcat, *gs, *prevs, *pars),
    )

    def swap(x, even, odd):
        return lax.ppermute(x, "tm", [(i, i ^ (odd if i % 2 else even)) for i in range(n_tm)])

    mine = [kp] + [swap(kp, *m) for m in CROSS]
    aprev = lax.ppermute(a, "tm", chain)
    plan = local_plan(count)[0]
    w_late, _ = lax.optimization_barrier((wcat, kp))
    near_part = call(
        functools.partial(local_kernel, count, n_g, n_par),
        shape(4, count, BV, LANES),
        scratch_for(plan),
        (aprev, w_late, *gs, *prevs, *pars),
        flops=5 << 30,
    )
    theirs, done = [], near_part
    for x in mine:
        done = swap(lax.optimization_barrier((x, done))[0], 1, 1)
        theirs.append(done)
    plan = final_plan(count, n_tm)[0]
    return call(
        functools.partial(final_kernel, count, n_tm, n_g, n_par),
        shape(16, BV, LANES),
        [pltpu.VMEM((n_tm - 1, 2, count, BV, LANES), F32), pltpu.SemaphoreType.DMA((n_tm,))] + scratch_for(plan),
        (near_part, late, f, wcat, *mine, *theirs, *gs, *prevs, *pars),
        unplaced=range(4, 4 + n_tm),
    )


def solution(mesh):
    spec = PartitionSpec
    in_specs = (
        spec("tm", None, "space"),
        spec(None, "space"),
        spec(),
        spec(None, "space"),
        spec(None, "space"),
        spec(None, "space"),
    )
    return jax.shard_map(
        shards, mesh=mesh, in_specs=in_specs, out_specs=spec("tm", None, "space"), check_vma=False
    )
```
